512 devices in a mesh: src: 16 (over y, x_lo, core), dst: 32 (over x_hi, z).
Axes of the slice: x: 4 (x_hi: 2, x_lo: 2; x = x_hi * 2 + x_lo), y: 4, z: 16, core: 2. Of those that a mesh axis runs over, the one named last changes fastest.
Arguments:
- messages: bfloat16 [262144, 1024], P(('src', 'dst')), may hold values from -16 to 16
- edge_count: int32 [512], P(('src', 'dst')), may hold values from 1 to 512, 163840 in all
- reverse: int32 [512, 512], P(('src', 'dst')), may hold values from 0 to 511, as said below
- target_atom: int32 [262144], P(('src', 'dst')), may hold values from 0 to 127
- pair_target: int32 [512, 16], P(('src', 'dst')), may hold values from 0 to 3
- pair_source: int32 [512, 16], P(('src', 'dst')), may hold values from 0 to 127, as said below
- pair_count: int32 [512], P(('src', 'dst')), may hold values from 1 to 16, 5120 in all
- basis_blocks: bfloat16 [8192, 3, 128, 128], P(('src', 'dst')), may hold values from -0.5 to 0.5
- trip_weight: bfloat16 [1024, 128], replicated, may hold values from -0.1875 to 0.1875
- up_weight: bfloat16 [512, 1024], replicated, may hold values from -0.25 to 0.25
- atom_first: bfloat16 [1024, 1024], P(None, 'dst'), may hold values from -0.1875 to 0.1875
- atom_second: bfloat16 [1024, 1024], P(None, 'dst'), may hold values from -0.375 to 0.375
Outputs:
- updated: bfloat16 [262144, 1024], P(('src', 'dst'))
The draws below stay inside these ranges and needn't reach their ends.
Inputs may be any that keep to these rules, and one draw needn't show every extreme that they name: Row g pairs the slots of device g: reverse[g, reverse[g, e]] = e and reverse[g, e] != e. `edge_count`: some device has all 512 slots live. `pair_count`: some device has all 16 pairs live. `pair_source`: of one device's 16 pairs, at most 2 read blocks held by any one device of its source tile (block b is held by the device of dst index b // 4), and every holder that is read is read by exactly 2.
All inputs are finite; a program needn't handle non-finite values.
Results may differ from the reference program's by a relative error of at most 0.0055.
Values may be sent and summed in bfloat16 or wider, within the bound.
No kernel may reach another device: no remote copies, remote signals or barrier semaphores. Data moves between devices by JAX's collectives and lax.ppermute only.
A program may use at most 64 MiB of HBM per device.

```python
import math
import jax
import jax.numpy as jnp
import numpy as np
from jax import lax

D = 1024
TRIP = 128
BLOCK = 128
A_DST = 128
E_DEV = 512
NP = 16
NBL = 4
EDGES = 262144
N_SRC = 16
N_DST = 32


def draw_messages(key, part):
    first, second, third = jax.random.split(key, 3)
    total_rows = E_DEV * N_SRC * N_DST
    base = jax.random.normal(first, (total_rows, D), jnp.float32)
    columns = jnp.exp(jax.random.uniform(second, (1, D), jnp.float32, math.log(0.3), math.log(3.0)))
    rows = jnp.exp(jax.random.uniform(third, (total_rows, 1), jnp.float32, math.log(0.5), math.log(2.0)))
    tile_of_row = (jnp.arange(total_rows, dtype=jnp.int32) // (E_DEV * N_DST)).astype(jnp.float32)
    rising = 0.3 * jnp.exp(math.log(10.0) * tile_of_row / max(N_SRC - 1, 1))
    rows = rows * rising[:, None]
    values = base * columns * rows
    return jnp.clip(values, -16.0, 16.0).astype(jnp.bfloat16)


def draw_reverse(key, part):
    keys = jax.random.split(jax.random.fold_in(key, 11), N_SRC * N_DST)

    def single(subkey):
        order = jax.random.permutation(subkey, E_DEV).astype(jnp.int32)
        place = jnp.zeros((E_DEV,), jnp.int32).at[order].set(jnp.arange(E_DEV, dtype=jnp.int32))
        return order[jnp.bitwise_xor(place, 1)]
    return jax.vmap(single)(keys)


def draw_pair_source(key, part):
    keys = jax.random.split(jax.random.fold_in(key, 23), N_SRC * N_DST)

    def single(subkey):
        first, second, third = jax.random.split(subkey, 3)
        holders = jax.random.permutation(first, N_DST).astype(jnp.int32)[:NP // 2]
        holders = jnp.repeat(holders, 2)
        shuffle = jax.random.permutation(second, NP).astype(jnp.int32)
        holders = holders[shuffle]
        local = jax.random.randint(third, (NP,), 0, NBL, dtype=jnp.int32)
        return holders * NBL + local
    return jax.vmap(single)(keys)


def with_ends(array, key, smallest, high):
    spot = [jax.random.randint(jax.random.fold_in(key, axis), (), 0, length) for axis, length in enumerate(array.shape)]
    longest = array.shape.index(max(array.shape))
    neighbour = spot[:longest] + [(spot[longest] + 1) % array.shape[longest]] + spot[longest + 1:]
    return array.at[tuple(spot)].set(smallest).at[tuple(neighbour)].set(high)


def levels(key, shape, cuts, low, largest):
    factor_of, own = 1.0, jax.random.fold_in(key, 6)
    for dim, parts in cuts:
        heights = jnp.exp(jax.random.uniform(jax.random.fold_in(own, dim), (parts,), jnp.float32, low / len(cuts), largest / len(cuts)))
        factor_of = factor_of * jnp.repeat(heights, shape[dim] // parts).reshape([-1 if axis == dim else 1 for axis in range(len(shape))])
    return factor_of


def split_up(amount, total, bound, slope):
    portions = [(1 << 20) // math.isqrt(rank ** slope) + 1 for rank in range(2, amount + 1)]
    surplus, holding = total - bound - (amount - 1), [1] * (amount - 1)
    while surplus > 0:
        candidates = [i for i in range(amount - 1) if holding[i] < bound]
        mass, budget = sum([portions[i] for i in candidates]), surplus
        for i in candidates:
            addition = min(bound - holding[i], max(1, budget * portions[i] // mass), surplus)
            holding[i] = holding[i] + addition
            surplus = surplus - addition
    return np.array([bound] + holding)


def ragged(own_key, amount, total, reach, skew):
    if amount == 2:
        one = jax.random.randint(own_key, (), max(1, total - reach), min(reach, total - 1) + 1)
        return jnp.stack([one, total - one])
    lengths = jnp.asarray(split_up(amount, total, reach, skew), jnp.int32)
    couples = (amount - 1) // 2
    giver, receiver = lengths[1:1 + 2 * couples:2], lengths[2:2 + 2 * couples:2]
    room = jnp.minimum(giver - 1, reach - receiver)
    shifted = jax.random.randint(jax.random.fold_in(own_key, 1), (couples,), 0, 1 << 20) % (room + 1)
    lengths = lengths.at[1:1 + 2 * couples:2].set(giver - shifted).at[2:2 + 2 * couples:2].set(receiver + shifted)
    return lengths[jax.random.permutation(jax.random.fold_in(own_key, 2), amount)]


def bell_draw(key, shape, scale, limit, cuts=(), kind=jnp.bfloat16):
    factor_of = levels(key, shape, cuts, -0.22, 0.18) if cuts else 1.0
    values = jax.random.normal(key, shape, jnp.float32) * scale * factor_of
    return jnp.minimum(jnp.maximum(values, -limit), limit).astype(kind)


def setup_inputs(seed: int = 0) -> dict:
    streams_of = jax.random.split(jax.random.key(seed), 13)
    return {
        "messages": draw_messages(jax.random.fold_in(streams_of[12], 71), 0),
        "edge_count": ragged(streams_of[1], N_SRC * N_DST, N_SRC * N_DST * E_DEV * 5 // 8, E_DEV, 2).astype(jnp.int32),
        "reverse": draw_reverse(jax.random.fold_in(streams_of[12], 71), 0),
        "target_atom": with_ends(jax.random.randint(streams_of[3], (EDGES,), 0, A_DST), jax.random.fold_in(streams_of[3], 1), 0, A_DST - 1).astype(jnp.int32),
        "pair_target": with_ends(jax.random.randint(streams_of[4], (N_SRC * N_DST, NP), 0, NBL), jax.random.fold_in(streams_of[4], 1), 0, NBL - 1).astype(jnp.int32),
        "pair_source": draw_pair_source(jax.random.fold_in(streams_of[12], 71), 0),
        "pair_count": ragged(streams_of[6], N_SRC * N_DST, N_SRC * N_DST * NP * 5 // 8, NP, 2).astype(jnp.int32),
        "basis_blocks": bell_draw(streams_of[7], (N_SRC * N_DST * NP, 3, BLOCK, BLOCK), BLOCK ** -0.5, 0.5, ((0, 512),)),
        "trip_weight": bell_draw(streams_of[8], (D, TRIP), D ** -0.5, 0.1875),
        "up_weight": bell_draw(streams_of[9], (4 * TRIP, D), (4 * TRIP) ** -0.5, 0.25),
        "atom_first": bell_draw(streams_of[10], (D, D), D ** -0.5, 0.1875, ((1, 32),)),
        "atom_second": bell_draw(streams_of[11], (D, D), (D // 4) ** -0.5, 0.375, ((1, 32),)),
    }


eps = 1e-06

def layer(act, weight, squash):
    out = jnp.dot(act, weight, preferred_element_type=jnp.float32)
    if squash:
        out = jax.nn.silu(out)
    return out.astype(jnp.bfloat16)

def reference(messages, edge_count, reverse, target_atom, pair_target, pair_source, pair_count, basis_blocks, trip_weight, up_weight, atom_first, atom_second):
    devices = N_SRC * N_DST
    positions = jnp.arange(E_DEV, dtype=jnp.int32)
    live_rows = positions[None, :] < edge_count[:, None]
    masked = jnp.where(live_rows.reshape(-1)[:, None], messages, jnp.zeros((), jnp.bfloat16))
    projected = jnp.dot(masked, trip_weight, preferred_element_type=jnp.float32).astype(jnp.bfloat16)
    row_blocks = projected.reshape(N_SRC, N_DST * E_DEV // BLOCK, BLOCK, TRIP)
    grouped = masked.reshape(N_SRC, N_DST, E_DEV, D)
    targets = target_atom.reshape(N_SRC, N_DST, E_DEV)
    atom_ids = jnp.arange(A_DST, dtype=jnp.int32)

    def tile_sum(column):
        rows = lax.dynamic_index_in_dim(grouped, column, 1, keepdims=False).reshape(-1, D)
        ids = lax.dynamic_index_in_dim(targets, column, 1, keepdims=False).reshape(-1)
        one_hot = (ids[:, None] == atom_ids[None, :]).astype(jnp.bfloat16)
        return lax.dot_general(one_hot, rows, (((0,), (0,)), ((), ())), preferred_element_type=jnp.float32)
    sums = lax.map(tile_sum, jnp.arange(N_DST, dtype=jnp.int32)).reshape(-1, D)
    scale = lax.rsqrt(lax.optimization_barrier(jnp.mean(sums * sums, axis=-1, keepdims=True)) + eps)
    normed = jax.nn.silu(sums * scale).astype(jnp.bfloat16)
    hidden = layer(normed, atom_first, True)
    atoms = layer(hidden, atom_second, False).reshape(N_DST, A_DST, D)
    bases = basis_blocks.reshape(devices, NP, 3, BLOCK, BLOCK)
    pair_ids = jnp.arange(NP, dtype=jnp.int32)
    block_ids = jnp.arange(E_DEV // BLOCK, dtype=jnp.int32)

    def update(index):
        row = index // N_DST
        column = index % N_DST
        start = index * E_DEV
        own = lax.dynamic_slice_in_dim(messages, start, E_DEV, 0)
        live = lax.dynamic_index_in_dim(live_rows, index, 0, keepdims=False)
        mine = lax.dynamic_slice_in_dim(projected, start, E_DEV, 0)
        blocks_row = lax.dynamic_index_in_dim(row_blocks, row, 0, keepdims=False)
        sources = lax.dynamic_index_in_dim(pair_source, index, 0, keepdims=False)
        chosen = jnp.take(blocks_row, sources, axis=0).astype(jnp.float32)
        basis = lax.dynamic_index_in_dim(bases, index, 0, keepdims=False).astype(jnp.float32)
        products = jnp.einsum('pkij,pjt->pikt', basis, chosen, precision=lax.Precision.HIGHEST)
        pair_live = pair_ids < lax.dynamic_index_in_dim(pair_count, index, 0, keepdims=False)
        goals = lax.dynamic_index_in_dim(pair_target, index, 0, keepdims=False)
        placing = ((goals[:, None] == block_ids[None, :]) & pair_live[:, None]).astype(jnp.float32)
        triplet = jnp.einsum('pb,pikt->bikt', placing, products, precision=lax.Precision.HIGHEST)
        triplet = triplet.reshape(E_DEV, 3 * TRIP).astype(jnp.bfloat16)
        mirrored = jnp.take(mine, lax.dynamic_index_in_dim(reverse, index, 0, keepdims=False), axis=0)
        tile_atoms = lax.dynamic_index_in_dim(atoms, column, 0, keepdims=False)
        ids = lax.dynamic_slice_in_dim(target_atom, start, E_DEV, 0)
        one_hot = (ids[:, None] == atom_ids[None, :]).astype(jnp.bfloat16)
        joined = jnp.concatenate([triplet, mirrored], axis=1)
        edge_input = jnp.dot(joined, up_weight, preferred_element_type=jnp.float32)
        edge_input = edge_input + jnp.dot(one_hot, tile_atoms, preferred_element_type=jnp.float32)
        result = own.astype(jnp.float32) + jax.nn.silu(edge_input)
        return jnp.where(live[:, None], result, jnp.zeros((), jnp.float32)).astype(jnp.bfloat16)
    return lax.map(update, jnp.arange(devices, dtype=jnp.int32)).reshape(-1, D)
```

```python
import jax
import jax.numpy as jnp
from jax import lax
from jax.experimental import pallas as pl
from jax.experimental.pallas import tpu as pltpu
from jax.sharding import Mesh, PartitionSpec as P

A_DST = 128
BLOCK = 128
AXES = (("y", 4), ("xl", 2), ("c", 2), ("xh", 2), ("z", 16))
ALL = tuple(name for name, _ in AXES)
SRC = ("y", "xl", "c")
N_SRC = 16
N_XH = 2
N_Z = 16
SHIFTS = (0, 8, 1, 9, 15, 7, 2, 10, 14, 6, 3, 11, 13, 5, 4, 12)
HOLDERS = tuple(SHIFTS.index(s) for s in range(N_Z))
eps = 1e-06


def silu(values):
    return values / (1.0 + jnp.exp(-values))


def shift_pairs():
    return [
        (r * N_Z + (z + SHIFTS[r]) % N_Z, r * N_Z + z)
        for r in range(N_SRC)
        for z in range(N_Z)
    ]


def spread(block):
    copies = jnp.broadcast_to(block[None], (N_SRC, *block.shape))
    return lax.all_to_all(copies, SRC, split_axis=0, concat_axis=0, tiled=True)


def second_layer(order, hidden, weight):
    def kernel(order_ref, hidden_ref, weight_ref, out_ref, sorted_ref):
        width = hidden_ref.shape[2]
        for z in range(N_Z):
            r = order_ref[z]
            for half in range(N_XH):
                start = (half * N_Z + z) * width
                sorted_ref[start : start + width, :] = hidden_ref[r, half]
        out_ref[...] = jnp.dot(
            weight_ref[...], sorted_ref[...], preferred_element_type=jnp.float32
        ).astype(jnp.bfloat16)

    features = weight.shape[1]
    return pl.pallas_call(
        kernel,
        out_shape=jax.ShapeDtypeStruct((weight.shape[0], hidden.shape[3]), jnp.bfloat16),
        in_specs=[
            pl.BlockSpec(memory_space=pltpu.SMEM),
            pl.BlockSpec(memory_space=pltpu.VMEM),
            pl.BlockSpec(memory_space=pltpu.VMEM),
        ],
        out_specs=pl.BlockSpec(memory_space=pltpu.VMEM),
        scratch_shapes=[pltpu.VMEM((features, hidden.shape[3]), jnp.bfloat16)],
        cost_estimate=pl.CostEstimate(
            flops=2 * 64 * 128 * 1024, bytes_accessed=500_000, transcendentals=0
        ),
        name="second_layer",
    )(order, hidden, weight)


def finish_kernel(
    scalars_ref,
    order_ref,
    rows_hbm,
    basis_hbm,
    up_hbm,
    atoms_hbm,
    mirrored_hbm,
    targets_hbm,
    messages_hbm,
    out_hbm,
    rows,
    basis,
    up,
    atoms,
    atoms_sorted,
    mirrored,
    targets,
    messages,
    triplet,
    result,
    row_sem,
    basis_sem,
    sems,
    message_sem,
    out_sem,
):
    pairs, kinds = basis.shape[0], basis.shape[1]
    edges = messages.shape[0]
    blocks = edges // BLOCK

    def source(p):
        block = scalars_ref[pairs + p]
        holder, local = block // blocks, block % blocks
        return ((holder % N_Z) * N_XH + holder // N_Z) * blocks + local

    row_copies = [
        pltpu.make_async_copy(rows_hbm.at[source(p)], rows.at[p], row_sem.at[p])
        for p in range(pairs)
    ]
    basis_copies = [
        pltpu.make_async_copy(basis_hbm.at[p], basis.at[p], basis_sem.at[p])
        for p in range(pairs)
    ]
    others = [
        pltpu.make_async_copy(src, dst, sems.at[i])
        for i, (src, dst) in enumerate(
            (
                (up_hbm, up),
                (atoms_hbm, atoms),
                (mirrored_hbm, mirrored),
                (targets_hbm, targets),
            )
        )
    ]
    message_copies = [
        pltpu.make_async_copy(
            messages_hbm.at[pl.ds(b * BLOCK, BLOCK)],
            messages.at[pl.ds(b * BLOCK, BLOCK)],
            message_sem.at[b],
        )
        for b in range(blocks)
    ]
    for p in range(pairs):
        row_copies[p].start()
        basis_copies[p].start()
    for copy in others + message_copies:
        copy.start()
    triplet[...] = jnp.zeros_like(triplet)
    for p in range(pairs):
        row_copies[p].wait()
        basis_copies[p].wait()

        @pl.when(p < scalars_ref[2 * pairs])
        def _():
            start = pl.multiple_of(scalars_ref[p] * BLOCK, BLOCK)
            product = jnp.dot(
                basis[p].reshape(kinds * BLOCK, BLOCK),
                rows[p],
                preferred_element_type=jnp.float32,
            )
            for k in range(kinds):
                triplet[pl.ds(start, BLOCK), k * BLOCK : (k + 1) * BLOCK] += product[
                    k * BLOCK : (k + 1) * BLOCK
                ]

    for copy in others:
        copy.wait()
    width = atoms.shape[2]
    for z in range(N_Z):
        r = order_ref[z]
        for half in range(N_XH):
            start = (half * N_Z + z) * width
            atoms_sorted[start : start + width, :] = atoms[r, half]
    live = scalars_ref[2 * pairs + 1]
    inner = kinds * BLOCK
    out_copies = []
    for b in range(blocks):
        span = pl.ds(b * BLOCK, BLOCK)
        edge_input = jnp.dot(
            triplet[span, :].astype(jnp.bfloat16), up[:inner, :], preferred_element_type=jnp.float32
        )
        edge_input += jnp.dot(mirrored[span, :], up[inner:, :], preferred_element_type=jnp.float32)
        atom_ids = lax.broadcasted_iota(jnp.int32, (A_DST, BLOCK), 0)
        hot = (atom_ids == targets[b : b + 1, :]).astype(jnp.float32).astype(jnp.bfloat16)
        edge_input += lax.dot_general(
            hot.T,
            atoms_sorted[...],
            (((1,), (1,)), ((), ())),
            preferred_element_type=jnp.float32,
        )
        message_copies[b].wait()
        total = messages[span, :].astype(jnp.float32) + silu(edge_input)
        positions = lax.broadcasted_iota(jnp.int32, total.shape, 0) + b * BLOCK
        result[span, :] = jnp.where(positions < live, total, 0.0).astype(jnp.bfloat16)
        copy = pltpu.make_async_copy(
            result.at[span], out_hbm.at[span], out_sem.at[b]
        )
        copy.start()
        out_copies.append(copy)
    for copy in out_copies:
        copy.wait()


def finish(scalars, order, rows, basis, up, atoms, mirrored, targets, messages):
    edges, width = messages.shape
    pairs, kinds = basis.shape[:2]
    blocks = edges // BLOCK
    anywhere = pl.BlockSpec(memory_space=pl.ANY)
    small = pl.BlockSpec(memory_space=pltpu.SMEM)
    return pl.pallas_call(
        finish_kernel,
        out_shape=jax.ShapeDtypeStruct((edges, width), jnp.bfloat16),
        in_specs=[small, small] + [anywhere] * 7,
        out_specs=anywhere,
        scratch_shapes=[
            pltpu.VMEM((pairs, BLOCK, BLOCK), jnp.bfloat16),
            pltpu.VMEM(basis.shape, jnp.bfloat16),
            pltpu.VMEM(up.shape, jnp.bfloat16),
            pltpu.VMEM(atoms.shape, jnp.bfloat16),
            pltpu.VMEM((width, A_DST), jnp.bfloat16),
            pltpu.VMEM(mirrored.shape, jnp.bfloat16),
            pltpu.VMEM(targets.shape, jnp.int32),
            pltpu.VMEM(messages.shape, jnp.bfloat16),
            pltpu.VMEM((edges, kinds * BLOCK), jnp.float32),
            pltpu.VMEM(messages.shape, jnp.bfloat16),
            pltpu.SemaphoreType.DMA((pairs,)),
            pltpu.SemaphoreType.DMA((pairs,)),
            pltpu.SemaphoreType.DMA((4,)),
            pltpu.SemaphoreType.DMA((blocks,)),
            pltpu.SemaphoreType.DMA((blocks,)),
        ],
        cost_estimate=pl.CostEstimate(
            flops=900_000_000, bytes_accessed=6_000_000, transcendentals=600_000
        ),
        name="finish",
    )(scalars, order, rows, basis, up, atoms, mirrored, targets, messages)


def on_device(
    messages,
    edge_count,
    reverse,
    target_atom,
    pair_target,
    pair_source,
    pair_count,
    basis_blocks,
    trip_weight,
    up_weight,
    atom_first,
    atom_second,
):
    edges = messages.shape[0]
    width = trip_weight.shape[1]
    live_rows = lax.broadcasted_iota(jnp.int32, (edges, 1), 0) < edge_count[0]
    masked = jnp.where(live_rows, messages, jnp.zeros((), jnp.bfloat16))
    projected = jnp.dot(masked, trip_weight, preferred_element_type=jnp.float32).astype(
        jnp.bfloat16
    )
    both = lax.all_gather(projected, "xh", axis=0, tiled=True)
    tile_rows = lax.all_gather(both, "z", axis=0, tiled=True)
    tile_blocks = tile_rows.reshape(-1, BLOCK, width)
    mine = jnp.concatenate([atom_first.T, atom_second.T], axis=0)
    mine, both = lax.optimization_barrier((mine, both))
    pair_of_columns = lax.all_gather(mine, "xh", axis=0)
    columns = lax.ppermute(pair_of_columns, (*SRC, "z"), shift_pairs())
    half = atom_first.shape[1]
    first = columns[:, :half].reshape(N_XH * half, -1)
    second = columns[:, half:].reshape(N_XH * half, -1)
    order = jnp.asarray(HOLDERS, jnp.int32)[
        jnp.mod(jnp.arange(N_Z, dtype=jnp.int32) - lax.axis_index("z"), N_Z)
    ]
    atom_ids = lax.broadcasted_iota(jnp.int32, (1, A_DST), 1)
    one_hot = (target_atom[:, None] == atom_ids).astype(jnp.bfloat16)
    local_sums = lax.dot_general(
        one_hot, masked, (((0,), (0,)), ((), ())), preferred_element_type=jnp.float32
    ).astype(jnp.bfloat16)
    parts = lax.all_to_all(local_sums, SRC, split_axis=0, concat_axis=0, tiled=True)
    sums = jnp.sum(parts.reshape(N_SRC, A_DST // N_SRC, -1).astype(jnp.float32), axis=0)
    scale = lax.rsqrt(jnp.mean(sums * sums, axis=-1, keepdims=True) + eps)
    normed = silu(sums * scale).astype(jnp.bfloat16)
    normed = spread(normed).reshape(A_DST, -1)
    hidden = lax.dot_general(
        first, normed, (((1,), (1,)), ((), ())), preferred_element_type=jnp.float32
    )
    hidden = silu(hidden).astype(jnp.bfloat16)
    hidden = spread(hidden).reshape(N_SRC, N_XH, half, A_DST)
    atoms = second_layer(order, hidden, second)
    atoms = spread(atoms).reshape(N_SRC, N_XH, half, A_DST)
    mirrored = jnp.take(projected, reverse[0], axis=0)
    scalars = jnp.concatenate([pair_target[0], pair_source[0], pair_count, edge_count])
    return finish(
        scalars,
        order,
        tile_blocks,
        basis_blocks,
        up_weight,
        atoms,
        mirrored,
        target_atom.reshape(edges // BLOCK, BLOCK),
        messages,
    )


def solution(mesh):
    split = Mesh(mesh.devices.reshape([n for _, n in AXES]), ALL)
    return jax.shard_map(
        on_device,
        mesh=split,
        in_specs=(
            P(ALL, None),
            P(ALL),
            P(ALL, None),
            P(ALL),
            P(ALL, None),
            P(ALL, None),
            P(ALL),
            P(ALL, None, None, None),
            P(),
            P(),
            P(None, ("xh", "z")),
            P(None, ("xh", "z")),
        ),
        out_specs=P(ALL, None),
        check_vma=False,
    )
```

```python
import jax
import jax.numpy as jnp
from jax import lax
from jax.experimental import pallas as pl
from jax.experimental.pallas import tpu as pltpu
from jax.sharding import Mesh, PartitionSpec as P

A_DST = 128
BLOCK = 128
AXES = (("y", 4), ("xl", 2), ("c", 2), ("xh", 2), ("z", 16))
ALL = tuple(name for name, _ in AXES)
SRC = ("y", "xl", "c")
N_SRC = 16
N_XH = 2
N_Z = 16
OWN = (0, 8, 1, -7, -1, 7, 2, -6, -2, 6, 3, -5, -3, 5, 4, -4)
OTHER = (4, -4, -1, 7, 1, -7, -2, 6, 2, -6, -3, 5, 3, -5, 0, 8)
eps = 1e-06


def silu(values):
    return values / (1.0 + jnp.exp(-values))


def own_pairs():
    return [
        (r * N_Z + (z + OWN[r]) % N_Z, r * N_Z + z) for r in range(N_SRC) for z in range(N_Z)
    ]


def other_pairs():
    return [
        ((r * N_XH + 1 - h) * N_Z + (z + OTHER[r]) % N_Z, (r * N_XH + h) * N_Z + z)
        for r in range(N_SRC)
        for h in range(N_XH)
        for z in range(N_Z)
    ]


def column_order():
    h, z = lax.axis_index("xh"), lax.axis_index("z")
    away = jnp.mod(jnp.arange(N_Z, dtype=jnp.int32) - z, N_Z)
    tables = [
        jnp.asarray([[s % N_Z for s in side].index(d) * 2 + i for d in range(N_Z)], jnp.int32)[away]
        for i, side in enumerate((OWN, OTHER))
    ]
    return jnp.where(h == 0, jnp.concatenate(tables), jnp.concatenate(tables[::-1]))


def spread(block):
    copies = jnp.broadcast_to(block[None], (N_SRC, *block.shape))
    return lax.all_to_all(copies, SRC, split_axis=0, concat_axis=0, tiled=True)


def second_layer(order, hidden, weight):
    def kernel(order_ref, hidden_ref, weight_ref, out_ref, sorted_ref):
        width = hidden_ref.shape[1]
        for i in range(N_XH * N_Z):
            sorted_ref[i * width : (i + 1) * width, :] = hidden_ref[order_ref[i]]
        out_ref[...] = jnp.dot(
            weight_ref[...], sorted_ref[...], preferred_element_type=jnp.float32
        ).astype(jnp.bfloat16)

    atoms = hidden.shape[2]
    return pl.pallas_call(
        kernel,
        out_shape=jax.ShapeDtypeStruct((weight.shape[0], atoms), jnp.bfloat16),
        in_specs=[
            pl.BlockSpec(memory_space=pltpu.SMEM),
            pl.BlockSpec(memory_space=pltpu.VMEM),
            pl.BlockSpec(memory_space=pltpu.VMEM),
        ],
        out_specs=pl.BlockSpec(memory_space=pltpu.VMEM),
        scratch_shapes=[pltpu.VMEM((weight.shape[1], atoms), jnp.bfloat16)],
        cost_estimate=pl.CostEstimate(
            flops=2 * 64 * 128 * 1024, bytes_accessed=500_000, transcendentals=0
        ),
        name="second_layer",
    )(order, hidden, weight)


def finish_kernel(
    scalars_ref,
    order_ref,
    rows_hbm,
    basis_hbm,
    up_hbm,
    atoms_hbm,
    mirrored_hbm,
    targets_hbm,
    messages_hbm,
    out_hbm,
    rows,
    basis,
    up,
    atoms,
    atoms_sorted,
    mirrored,
    targets,
    messages,
    placed,
    hot,
    triplet,
    result,
    row_sem,
    basis_sem,
    sems,
    out_sem,
):
    pairs, kinds = basis.shape[0], basis.shape[1]
    edges, width = messages.shape
    blocks = edges // BLOCK

    def source(p):
        block = scalars_ref[pairs + p]
        holder, local = block // blocks, block % blocks
        return ((holder % N_Z) * N_XH + holder // N_Z) * blocks + local

    row_copies = [
        pltpu.make_async_copy(rows_hbm.at[source(p)], rows.at[p], row_sem.at[p])
        for p in range(pairs)
    ]
    basis_copies = [
        pltpu.make_async_copy(basis_hbm.at[p], basis.at[p], basis_sem.at[p])
        for p in range(pairs)
    ]
    small_copies = [
        pltpu.make_async_copy(src, dst, sems.at[i])
        for i, (src, dst) in enumerate(
            (
                (targets_hbm, targets),
                (atoms_hbm, atoms),
                (mirrored_hbm, mirrored),
                (up_hbm, up),
                (messages_hbm, messages),
            )
        )
    ]
    for copy in small_copies[:3]:
        copy.start()
    for p in range(pairs):
        row_copies[p].start()
        basis_copies[p].start()
    for copy in small_copies[3:]:
        copy.start()

    small_copies[0].wait()
    atom_ids = lax.broadcasted_iota(jnp.int32, (A_DST, BLOCK), 0)
    for b in range(blocks):
        flags = (atom_ids == targets[b : b + 1, :]).astype(jnp.float32)
        hot[b * BLOCK : (b + 1) * BLOCK, :] = flags.T.astype(jnp.bfloat16)
    small_copies[1].wait()
    half = atoms.shape[1]
    for i in range(N_XH * N_Z):
        atoms_sorted[i * half : (i + 1) * half, :] = atoms[order_ref[i]]

    count = scalars_ref[2 * pairs]
    for p in range(pairs):
        row_copies[p].wait()
        goal = jnp.where(p < count, scalars_ref[p], -1)
        for b in range(blocks):
            chosen = jnp.where(goal == b, rows[p], jnp.zeros((), jnp.bfloat16))
            placed[p * BLOCK : (p + 1) * BLOCK, b * BLOCK : (b + 1) * BLOCK] = chosen
    for copy in basis_copies:
        copy.wait()
    for k in range(kinds):
        factors = jnp.concatenate([basis[p, k] for p in range(pairs)], axis=1)
        sums = jnp.dot(factors, placed[...], preferred_element_type=jnp.float32)
        for b in range(blocks):
            triplet[b * BLOCK : (b + 1) * BLOCK, k * BLOCK : (k + 1) * BLOCK] = sums[
                :, b * BLOCK : (b + 1) * BLOCK
            ].astype(jnp.bfloat16)
    for copy in small_copies[2:]:
        copy.wait()

    live = scalars_ref[2 * pairs + 1]
    inner = kinds * BLOCK
    chunk = 256
    alive = lax.broadcasted_iota(jnp.int32, (edges, chunk), 0) < live
    out_copies = []
    for n in range(width // chunk):
        span = slice(n * chunk, (n + 1) * chunk)
        edge_input = jnp.dot(triplet[...], up[:inner, span], preferred_element_type=jnp.float32)
        edge_input += jnp.dot(mirrored[...], up[inner:, span], preferred_element_type=jnp.float32)
        edge_input += lax.dot_general(
            hot[...],
            atoms_sorted[span, :],
            (((1,), (1,)), ((), ())),
            preferred_element_type=jnp.float32,
        )
        total = messages[:, span].astype(jnp.float32) + silu(edge_input)
        result[:, span] = jnp.where(alive, total, 0.0).astype(jnp.bfloat16)
        copy = pltpu.make_async_copy(
            result.at[:, pl.ds(n * chunk, chunk)],
            out_hbm.at[:, pl.ds(n * chunk, chunk)],
            out_sem.at[n],
        )
        copy.start()
        out_copies.append(copy)
    for copy in out_copies:
        copy.wait()


def finish(scalars, order, rows, basis, up, atoms, mirrored, targets, messages):
    edges, width = messages.shape
    pairs, kinds = basis.shape[:2]
    anywhere = pl.BlockSpec(memory_space=pl.ANY)
    small = pl.BlockSpec(memory_space=pltpu.SMEM)
    return pl.pallas_call(
        finish_kernel,
        out_shape=jax.ShapeDtypeStruct((edges, width), jnp.bfloat16),
        in_specs=[small, small] + [anywhere] * 7,
        out_specs=anywhere,
        scratch_shapes=[
            pltpu.VMEM((pairs, BLOCK, BLOCK), jnp.bfloat16),
            pltpu.VMEM(basis.shape, jnp.bfloat16),
            pltpu.VMEM(up.shape, jnp.bfloat16),
            pltpu.VMEM(atoms.shape, jnp.bfloat16),
            pltpu.VMEM((width, A_DST), jnp.bfloat16),
            pltpu.VMEM(mirrored.shape, jnp.bfloat16),
            pltpu.VMEM(targets.shape, jnp.int32),
            pltpu.VMEM(messages.shape, jnp.bfloat16),
            pltpu.VMEM((pairs * BLOCK, edges), jnp.bfloat16),
            pltpu.VMEM((edges, A_DST), jnp.bfloat16),
            pltpu.VMEM((edges, kinds * BLOCK), jnp.bfloat16),
            pltpu.VMEM(messages.shape, jnp.bfloat16),
            pltpu.SemaphoreType.DMA((pairs,)),
            pltpu.SemaphoreType.DMA((pairs,)),
            pltpu.SemaphoreType.DMA((5,)),
            pltpu.SemaphoreType.DMA((4,)),
        ],
        cost_estimate=pl.CostEstimate(
            flops=900_000_000, bytes_accessed=6_000_000, transcendentals=600_000
        ),
        name="finish",
    )(scalars, order, rows, basis, up, atoms, mirrored, targets, messages)


def on_device(
    messages,
    edge_count,
    reverse,
    target_atom,
    pair_target,
    pair_source,
    pair_count,
    basis_blocks,
    trip_weight,
    up_weight,
    atom_first,
    atom_second,
):
    edges = messages.shape[0]
    width = trip_weight.shape[1]
    live_rows = lax.broadcasted_iota(jnp.int32, (edges, 1), 0) < edge_count[0]
    masked = jnp.where(live_rows, messages, jnp.zeros((), jnp.bfloat16))
    projected = jnp.dot(masked, trip_weight, preferred_element_type=jnp.float32).astype(
        jnp.bfloat16
    )
    both = lax.all_gather(projected, "xh", axis=0, tiled=True)
    tile_rows = lax.all_gather(both, "z", axis=0, tiled=True)
    tile_blocks = tile_rows.reshape(-1, BLOCK, width)
    half = atom_first.shape[1]
    mine = jnp.concatenate([atom_first.T, atom_second.T], axis=0)
    mine, both = lax.optimization_barrier((mine, both))
    own = lax.ppermute(mine, (*SRC, "z"), own_pairs())
    other = lax.ppermute(mine, ALL, other_pairs())
    first = jnp.concatenate([own[:half], other[:half]], axis=0)
    second = jnp.concatenate([own[half:], other[half:]], axis=0)
    order = column_order()
    atom_ids = lax.broadcasted_iota(jnp.int32, (1, A_DST), 1)
    one_hot = (target_atom[:, None] == atom_ids).astype(jnp.bfloat16)
    local_sums = lax.dot_general(
        one_hot, masked, (((0,), (0,)), ((), ())), preferred_element_type=jnp.float32
    ).astype(jnp.bfloat16)
    parts = lax.all_to_all(local_sums, SRC, split_axis=0, concat_axis=0, tiled=True)
    sums = jnp.sum(parts.reshape(N_SRC, A_DST // N_SRC, -1).astype(jnp.float32), axis=0)
    scale = lax.rsqrt(jnp.mean(sums * sums, axis=-1, keepdims=True) + eps)
    normed = silu(sums * scale).astype(jnp.bfloat16)
    normed = spread(normed).reshape(A_DST, -1)
    hidden = lax.dot_general(
        first, normed, (((1,), (1,)), ((), ())), preferred_element_type=jnp.float32
    )
    hidden = silu(hidden).astype(jnp.bfloat16)
    hidden = spread(hidden).reshape(N_SRC * N_XH, half, A_DST)
    atoms = second_layer(order, hidden, second)
    atoms = spread(atoms).reshape(N_SRC * N_XH, half, A_DST)
    mirrored = jnp.take(projected, reverse[0], axis=0)
    scalars = jnp.concatenate([pair_target[0], pair_source[0], pair_count, edge_count])
    return finish(
        scalars,
        order,
        tile_blocks,
        basis_blocks,
        up_weight,
        atoms,
        mirrored,
        target_atom.reshape(edges // BLOCK, BLOCK),
        messages,
    )


def solution(mesh):
    split = Mesh(mesh.devices.reshape([n for _, n in AXES]), ALL)
    return jax.shard_map(
        on_device,
        mesh=split,
        in_specs=(
            P(ALL, None),
            P(ALL),
            P(ALL, None),
            P(ALL),
            P(ALL, None),
            P(ALL, None),
            P(ALL),
            P(ALL, None, None, None),
            P(),
            P(),
            P(None, ("xh", "z")),
            P(None, ("xh", "z")),
        ),
        out_specs=P(ALL, None),
        check_vma=False,
    )
```

```python
import jax
import jax.numpy as jnp
from jax import lax
from jax.experimental import pallas as pl
from jax.experimental.pallas import tpu as pltpu
from jax.sharding import Mesh, PartitionSpec as P

A_DST = 128
BLOCK = 128
CHUNK = 256
ROWS = 64
AXES = (("y", 4), ("xl", 2), ("c", 2), ("xh", 2), ("z", 16))
ALL = tuple(name for name, _ in AXES)
SRC = ("y", "xl", "c")
N_SRC = 16
N_XH = 2
N_Z = 16
SHIFTS = (0, 8, 1, -7, -1, 7, 2, -6, -2, 6, 3, -5, -3, 5, 4, -4)
HOLDERS = tuple([s % N_Z for s in SHIFTS].index(d) for d in range(N_Z))
SHARERS = ("xh", *SRC)
eps = 1e-06


def silu(values):
    return values / (1.0 + jnp.exp(-values))


def shift_pairs():
    return [
        (r * N_Z + (z + SHIFTS[r]) % N_Z, r * N_Z + z) for r in range(N_SRC) for z in range(N_Z)
    ]


def column_order():
    away = jnp.mod(jnp.arange(N_Z, dtype=jnp.int32) - lax.axis_index("z"), N_Z)
    holders = jnp.asarray(HOLDERS, jnp.int32)[away]
    return jnp.concatenate([holders + h * N_SRC for h in range(N_XH)])


def exchange(blocks, axes):
    return lax.all_to_all(blocks, axes, split_axis=0, concat_axis=0, tiled=True)


def spread(block):
    return exchange(jnp.broadcast_to(block[None], (N_XH * N_SRC, *block.shape)), SHARERS)


def second_layer(order, hidden, weight):
    def kernel(order_ref, hidden_ref, weight_ref, out_ref, sorted_ref):
        width = hidden_ref.shape[1]
        for i in range(N_XH * N_Z):
            sorted_ref[i * width : (i + 1) * width, :] = hidden_ref[order_ref[i]]
        out = jnp.dot(weight_ref[...], sorted_ref[...], preferred_element_type=jnp.float32).astype(
            jnp.bfloat16
        )
        for h in range(N_XH):
            out_ref[h] = out[:, h * A_DST : (h + 1) * A_DST]

    columns, features = weight.shape
    return pl.pallas_call(
        kernel,
        out_shape=jax.ShapeDtypeStruct((N_XH, columns, A_DST), jnp.bfloat16),
        in_specs=[
            pl.BlockSpec(memory_space=pltpu.SMEM),
            pl.BlockSpec(memory_space=pltpu.VMEM),
            pl.BlockSpec(memory_space=pltpu.VMEM),
        ],
        out_specs=pl.BlockSpec(memory_space=pltpu.VMEM),
        scratch_shapes=[pltpu.VMEM((features, N_XH * A_DST), jnp.bfloat16)],
        cost_estimate=pl.CostEstimate(
            flops=2 * 32 * 256 * 1024, bytes_accessed=700_000, transcendentals=0
        ),
        name="second_layer",
    )(order, hidden, weight)


def edge_part(order, atoms, mirrored, targets, up):
    def kernel(order_ref, atoms_ref, mirrored_ref, targets_ref, up_ref, out_ref, sorted_ref, hot):
        half = atoms_ref.shape[1]
        edges, width = out_ref.shape
        for i in range(N_XH * N_Z):
            sorted_ref[i * half : (i + 1) * half, :] = atoms_ref[order_ref[i]]
        atom_ids = lax.broadcasted_iota(jnp.int32, (A_DST, BLOCK), 0)
        for b in range(edges // BLOCK):
            flags = (atom_ids == targets_ref[b : b + 1, :]).astype(jnp.float32)
            hot[b * BLOCK : (b + 1) * BLOCK, :] = flags.T.astype(jnp.bfloat16)
        for n in range(width // CHUNK):
            span = slice(n * CHUNK, (n + 1) * CHUNK)
            part = jnp.dot(mirrored_ref[...], up_ref[:, span], preferred_element_type=jnp.float32)
            part += lax.dot_general(
                hot[...],
                sorted_ref[span, :],
                (((1,), (1,)), ((), ())),
                preferred_element_type=jnp.float32,
            )
            out_ref[:, span] = 0.5 * part

    edges, width = mirrored.shape[0], up.shape[1]
    vmem = pl.BlockSpec(memory_space=pltpu.VMEM)
    return pl.pallas_call(
        kernel,
        out_shape=jax.ShapeDtypeStruct((edges, width), jnp.float32),
        in_specs=[pl.BlockSpec(memory_space=pltpu.SMEM)] + [vmem] * 4,
        out_specs=vmem,
        scratch_shapes=[
            pltpu.VMEM((width, A_DST), jnp.bfloat16),
            pltpu.VMEM((edges, A_DST), jnp.bfloat16),
        ],
        cost_estimate=pl.CostEstimate(
            flops=270_000_000, bytes_accessed=3_000_000, transcendentals=0
        ),
        name="edge_part",
    )(order, atoms, mirrored, targets, up)


def finish_kernel(
    scalars_ref,
    rows_hbm,
    basis_hbm,
    up_hbm,
    part_hbm,
    messages_hbm,
    out_hbm,
    basis,
    up,
    part,
    messages,
    placed,
    sums,
    triplet,
    product,
    fresh,
    result,
    row_sem,
    basis_sem,
    up_sem,
    part_sem,
    message_sem,
    out_sem,
):
    pairs, kinds = basis.shape[0], basis.shape[1]
    edges, width = messages.shape
    chunks = width // CHUNK

    row_copies = [
        pltpu.make_async_copy(
            rows_hbm.at[scalars_ref[pairs + p]],
            placed.at[pl.ds(p * BLOCK, BLOCK), pl.ds(p % 2 * BLOCK, BLOCK)],
            row_sem.at[p],
        )
        for p in range(pairs)
    ]
    basis_copy = pltpu.make_async_copy(basis_hbm, basis, basis_sem)
    up_copy = pltpu.make_async_copy(up_hbm, up, up_sem)
    spans = [pl.ds(n * CHUNK, CHUNK) for n in range(chunks)]
    part_copies = [
        pltpu.make_async_copy(part_hbm.at[:, s], part.at[:, s], part_sem.at[n])
        for n, s in enumerate(spans)
    ]
    message_copies = [
        pltpu.make_async_copy(messages_hbm.at[:, s], messages.at[:, s], message_sem.at[n])
        for n, s in enumerate(spans)
    ]
    basis_copy.start()
    for copy in row_copies:
        copy.start()
    up_copy.start()
    for first, second in zip(part_copies, message_copies):
        first.start()
        second.start()
    for p in range(pairs):
        off = (1 - p % 2) * BLOCK
        placed[p * BLOCK : (p + 1) * BLOCK, off : off + BLOCK] = jnp.zeros(
            (BLOCK, BLOCK), jnp.bfloat16
        )
    sums[...] = jnp.zeros_like(sums)

    basis_copy.wait()
    for copy in row_copies:
        copy.wait()
    for q in range(pairs // 2):
        factors = jnp.concatenate(
            [
                basis[2 * q].reshape(kinds * BLOCK, BLOCK),
                basis[2 * q + 1].reshape(kinds * BLOCK, BLOCK),
            ],
            axis=1,
        )
        product[q % 2] = jnp.dot(
            factors, placed[2 * q * BLOCK : 2 * (q + 1) * BLOCK, :], preferred_element_type=jnp.float32
        )
        for i in range(2):
            start = pl.multiple_of(scalars_ref[2 * q + i], BLOCK)
            for k in range(kinds):
                sums[pl.ds(start, BLOCK), k * BLOCK : (k + 1) * BLOCK] += product[
                    q % 2, k * BLOCK : (k + 1) * BLOCK, i * BLOCK : (i + 1) * BLOCK
                ]
    triplet[...] = sums[:edges, :].astype(jnp.bfloat16)

    for copy in [up_copy, *part_copies, *message_copies]:
        copy.wait()
    live = scalars_ref[2 * pairs]
    out_copies = []
    for n in range(chunks):
        span = slice(n * CHUNK, (n + 1) * CHUNK)
        fresh[n % 2] = jnp.dot(triplet[...], up[:, span], preferred_element_type=jnp.float32)
        for b in range(edges // ROWS):
            rows = slice(b * ROWS, (b + 1) * ROWS)
            low = fresh[n % 2, rows, :] + part[rows, span]
            total = (messages[rows, span].astype(jnp.float32) + low) + low * jnp.tanh(low)
            alive = lax.broadcasted_iota(jnp.int32, (ROWS, CHUNK), 0) < live - b * ROWS
            result[rows, span] = jnp.where(alive, total, 0.0).astype(jnp.bfloat16)
        copy = pltpu.make_async_copy(result.at[:, spans[n]], out_hbm.at[:, spans[n]], out_sem.at[n])
        copy.start()
        out_copies.append(copy)
    for copy in out_copies:
        copy.wait()


def finish(scalars, rows, basis, up, part, messages):
    edges, width = messages.shape
    pairs, kinds = basis.shape[:2]
    inner = kinds * BLOCK
    chunks = width // CHUNK
    anywhere = pl.BlockSpec(memory_space=pl.ANY)
    return pl.pallas_call(
        finish_kernel,
        out_shape=jax.ShapeDtypeStruct((edges, width), jnp.bfloat16),
        in_specs=[pl.BlockSpec(memory_space=pltpu.SMEM)] + [anywhere] * 5,
        out_specs=anywhere,
        scratch_shapes=[
            pltpu.VMEM(basis.shape, jnp.bfloat16),
            pltpu.VMEM((inner, width), jnp.bfloat16),
            pltpu.VMEM((edges, width), jnp.float32),
            pltpu.VMEM((edges, width), jnp.bfloat16),
            pltpu.VMEM((pairs * BLOCK, 2 * BLOCK), jnp.bfloat16),
            pltpu.VMEM((edges + BLOCK, inner), jnp.float32),
            pltpu.VMEM((edges, inner), jnp.bfloat16),
            pltpu.VMEM((2, inner, 2 * BLOCK), jnp.float32),
            pltpu.VMEM((2, edges, CHUNK), jnp.float32),
            pltpu.VMEM((edges, width), jnp.bfloat16),
            pltpu.SemaphoreType.DMA((pairs,)),
            pltpu.SemaphoreType.DMA,
            pltpu.SemaphoreType.DMA,
            pltpu.SemaphoreType.DMA((chunks,)),
            pltpu.SemaphoreType.DMA((chunks,)),
            pltpu.SemaphoreType.DMA((chunks,)),
        ],
        cost_estimate=pl.CostEstimate(
            flops=700_000_000, bytes_accessed=7_000_000, transcendentals=600_000
        ),
        name="finish",
    )(scalars, rows, basis, up, part, messages)


def on_device(
    messages,
    edge_count,
    reverse,
    target_atom,
    pair_target,
    pair_source,
    pair_count,
    basis_blocks,
    trip_weight,
    up_weight,
    atom_first,
    atom_second,
):
    edges = messages.shape[0]
    width = trip_weight.shape[1]
    live_rows = lax.broadcasted_iota(jnp.int32, (edges, 1), 0) < edge_count[0]
    masked = jnp.where(live_rows, messages, jnp.zeros((), jnp.bfloat16))
    projected = jnp.dot(masked, trip_weight, preferred_element_type=jnp.float32).astype(
        jnp.bfloat16
    )
    both = lax.all_gather(projected, "xh", axis=0, tiled=True)
    tile_rows = lax.all_gather(both, "z", axis=0, tiled=True)
    tile_blocks = tile_rows.reshape(-1, BLOCK, width)
    atom_ids = lax.broadcasted_iota(jnp.int32, (1, A_DST), 1)
    one_hot = (target_atom[:, None] == atom_ids).astype(jnp.bfloat16)
    local_sums = lax.dot_general(
        one_hot, masked, (((0,), (0,)), ((), ())), preferred_element_type=jnp.float32
    ).astype(jnp.bfloat16)
    columns = atom_first.shape[1]
    mine = jnp.concatenate([atom_first.T, atom_second.T], axis=0)
    mine, both, local_sums = lax.optimization_barrier((mine, both, local_sums))
    weights = lax.ppermute(mine, (*SRC, "z"), shift_pairs())
    first, second = weights[:columns], weights[columns:]
    order = column_order()
    parts = exchange(local_sums, SRC)
    sums = jnp.sum(parts.reshape(N_SRC, A_DST // N_SRC, -1).astype(jnp.float32), axis=0)
    scale = lax.rsqrt(jnp.mean(sums * sums, axis=-1, keepdims=True) + eps)
    normed = silu(sums * scale).astype(jnp.bfloat16)
    normed = spread(normed).reshape(N_XH * A_DST, -1)
    hidden = lax.dot_general(
        first, normed, (((1,), (1,)), ((), ())), preferred_element_type=jnp.float32
    )
    hidden = spread(silu(hidden).astype(jnp.bfloat16))
    atoms = second_layer(order, hidden, second)
    atoms = jnp.broadcast_to(atoms[:, None], (N_XH, N_SRC, columns, A_DST))
    atoms = exchange(atoms.reshape(-1, columns, A_DST), SHARERS)
    mirrored = jnp.take(projected, reverse[0], axis=0)
    blocks = edges // BLOCK
    inner = up_weight.shape[0] - width
    part = edge_part(
        order, atoms, mirrored, target_atom.reshape(blocks, BLOCK), up_weight[inner:]
    )
    half_up = up_weight[:inner] * jnp.asarray(0.5, jnp.bfloat16)
    pairs = pair_target.shape[1]
    live_pairs = jnp.arange(pairs, dtype=jnp.int32) < pair_count[0]
    starts = jnp.where(live_pairs, pair_target[0], blocks) * BLOCK
    holder, local = pair_source[0] // blocks, pair_source[0] % blocks
    sources = ((holder % N_Z) * N_XH + holder // N_Z) * blocks + local
    scalars = jnp.concatenate([starts, sources, edge_count])
    return finish(scalars, tile_blocks, basis_blocks, half_up, part, messages)


def solution(mesh):
    split = Mesh(mesh.devices.reshape([n for _, n in AXES]), ALL)
    return jax.shard_map(
        on_device,
        mesh=split,
        in_specs=(
            P(ALL, None),
            P(ALL),
            P(ALL, None),
            P(ALL),
            P(ALL, None),
            P(ALL, None),
            P(ALL),
            P(ALL, None, None, None),
            P(),
            P(),
            P(None, ("xh", "z")),
            P(None, ("xh", "z")),
        ),
        out_specs=P(ALL, None),
        check_vma=False,
    )
```

```python
import jax
import jax.numpy as jnp
from jax import lax
from jax.experimental import pallas as pl
from jax.experimental.pallas import tpu as pltpu
from jax.sharding import Mesh, PartitionSpec as P

A_DST = 128
BLOCK = 128
CHUNK = 256
ROWS = 64
AXES = (("y", 4), ("xl", 2), ("c", 2), ("xh", 2), ("z", 16))
ALL = tuple(name for name, _ in AXES)
SRC = ("y", "xl", "c")
N_SRC = 16
N_XH = 2
N_Z = 16
FIRST = (0, 8, 1, -7, -1, 7, 2, -6, -2, 6, 3, -5, -3, 5, 4, -4)
SECOND = (4, -4, -1, 7, 1, -7, -2, 6, 2, -6, -3, 5, 3, -5, 0, 8)
SHARERS = ("xh", *SRC)
eps = 1e-06


def silu(values):
    return values / (1.0 + jnp.exp(-values))


def shift_along_z(columns, shifts):
    pairs = [
        (r * N_Z + (z + shifts[r]) % N_Z, r * N_Z + z) for r in range(N_SRC) for z in range(N_Z)
    ]
    return lax.ppermute(columns, (*SRC, "z"), pairs)


def column_order(shifts):
    away = jnp.mod(jnp.arange(N_Z, dtype=jnp.int32) - lax.axis_index("z"), N_Z)
    places = [s % N_Z for s in shifts]
    holders = jnp.asarray([places.index(d) for d in range(N_Z)], jnp.int32)[away]
    return jnp.concatenate([holders + h * N_SRC for h in range(N_XH)])


def placed_in(space, *arrays):
    return [pltpu.with_memory_space_constraint(x, space) for x in arrays]


def exchange(blocks, axes):
    return lax.all_to_all(blocks, axes, split_axis=0, concat_axis=0, tiled=True)


def spread(block):
    return exchange(jnp.broadcast_to(block[None], (N_XH * N_SRC, *block.shape)), SHARERS)


def second_layer(order, hidden, weight):
    def kernel(order_ref, hidden_ref, weight_ref, out_ref, sorted_ref):
        width = hidden_ref.shape[1]
        for i in range(N_XH * N_Z):
            sorted_ref[i * width : (i + 1) * width, :] = hidden_ref[order_ref[i]]
        out = jnp.dot(weight_ref[...], sorted_ref[...], preferred_element_type=jnp.float32).astype(
            jnp.bfloat16
        )
        for h in range(N_XH):
            block = out[:, h * A_DST : (h + 1) * A_DST]
            for r in range(N_SRC):
                out_ref[h * N_SRC + r] = block

    columns, features = weight.shape
    vmem = pl.BlockSpec(memory_space=pltpu.VMEM)
    return pl.pallas_call(
        kernel,
        out_shape=jax.ShapeDtypeStruct((N_XH * N_SRC, columns, A_DST), jnp.bfloat16),
        in_specs=[pl.BlockSpec(memory_space=pltpu.SMEM), vmem, vmem],
        out_specs=vmem,
        scratch_shapes=[pltpu.VMEM((features, N_XH * A_DST), jnp.bfloat16)],
        cost_estimate=pl.CostEstimate(
            flops=2 * 32 * 256 * 1024, bytes_accessed=700_000, transcendentals=0
        ),
        compiler_params=pltpu.CompilerParams(vmem_limit_bytes=8 << 20),
        name="second_layer",
    )(order, *placed_in(pltpu.VMEM, hidden, weight))


def edge_part(order, atoms, mirrored, targets, up, basis):
    def kernel(
        order_ref,
        atoms_ref,
        mirrored_ref,
        targets_ref,
        up_ref,
        basis_hbm,
        out_hbm,
        basis_ref,
        sorted_ref,
        hot,
        part,
        basis_sem,
        sems,
    ):
        copies = [pltpu.make_async_copy(basis_hbm, basis_ref, basis_sem)]
        copies[0].start()
        half = atoms_ref.shape[1]
        edges, width = part.shape
        for i in range(N_XH * N_Z):
            sorted_ref[i * half : (i + 1) * half, :] = atoms_ref[order_ref[i]]
        atom_ids = lax.broadcasted_iota(jnp.int32, (A_DST, BLOCK), 0)
        for b in range(edges // BLOCK):
            flags = (atom_ids == targets_ref[b : b + 1, :]).astype(jnp.float32)
            hot[b * BLOCK : (b + 1) * BLOCK, :] = flags.T.astype(jnp.bfloat16)
        for n in range(width // CHUNK):
            span = slice(n * CHUNK, (n + 1) * CHUNK)
            both = jnp.dot(mirrored_ref[...], up_ref[:, span], preferred_element_type=jnp.float32)
            both += lax.dot_general(
                hot[...],
                sorted_ref[span, :],
                (((1,), (1,)), ((), ())),
                preferred_element_type=jnp.float32,
            )
            part[:, span] = 0.5 * both
            columns = pl.ds(n * CHUNK, CHUNK)
            copies.append(
                pltpu.make_async_copy(part.at[:, columns], out_hbm.at[:, columns], sems.at[n])
            )
            copies[-1].start()
        for copy in copies:
            copy.wait()

    edges, width = mirrored.shape[0], up.shape[1]
    vmem = pl.BlockSpec(memory_space=pltpu.VMEM)
    hbm = pl.BlockSpec(memory_space=pltpu.HBM)
    return pl.pallas_call(
        kernel,
        out_shape=(
            pltpu.HBM((edges, width), jnp.float32),
            pltpu.VMEM(basis.shape, basis.dtype),
        ),
        in_specs=[pl.BlockSpec(memory_space=pltpu.SMEM)] + [vmem] * 4 + [hbm],
        out_specs=(hbm, vmem),
        scratch_shapes=[
            pltpu.VMEM((width, A_DST), jnp.bfloat16),
            pltpu.VMEM((edges, A_DST), jnp.bfloat16),
            pltpu.VMEM((edges, width), jnp.float32),
            pltpu.SemaphoreType.DMA,
            pltpu.SemaphoreType.DMA((width // CHUNK,)),
        ],
        cost_estimate=pl.CostEstimate(
            flops=270_000_000, bytes_accessed=5_000_000, transcendentals=0
        ),
        compiler_params=pltpu.CompilerParams(vmem_limit_bytes=12 << 20),
        name="edge_part",
    )(
        order,
        *placed_in(pltpu.VMEM, atoms, mirrored),
        targets,
        up,
        *placed_in(pltpu.HBM, basis),
    )


def finish_kernel(
    scalars_ref,
    rows_hbm,
    part_hbm,
    messages_hbm,
    basis,
    up,
    out_hbm,
    part,
    messages,
    placed,
    sums,
    triplet,
    product,
    fresh,
    result,
    row_sem,
    part_sem,
    message_sem,
    out_sem,
):
    pairs, kinds = basis.shape[0], basis.shape[1]
    edges, width = messages.shape
    chunks = width // CHUNK

    row_copies = [
        pltpu.make_async_copy(
            rows_hbm.at[scalars_ref[pairs + p]],
            placed.at[pl.ds(p * BLOCK, BLOCK), pl.ds(p % 2 * BLOCK, BLOCK)],
            row_sem.at[p],
        )
        for p in range(pairs)
    ]
    spans = [pl.ds(n * CHUNK, CHUNK) for n in range(chunks)]
    part_copies = [
        pltpu.make_async_copy(part_hbm.at[:, s], part.at[:, s], part_sem.at[n])
        for n, s in enumerate(spans)
    ]
    message_copies = [
        pltpu.make_async_copy(messages_hbm.at[:, s], messages.at[:, s], message_sem.at[n])
        for n, s in enumerate(spans)
    ]
    for copy in row_copies:
        copy.start()
    for first, second in zip(part_copies, message_copies):
        first.start()
        second.start()
    for p in range(pairs):
        off = (1 - p % 2) * BLOCK
        placed[p * BLOCK : (p + 1) * BLOCK, off : off + BLOCK] = jnp.zeros(
            (BLOCK, BLOCK), jnp.bfloat16
        )
    sums[...] = jnp.zeros_like(sums)

    for copy in row_copies:
        copy.wait()
    for q in range(pairs // 2):
        factors = jnp.concatenate(
            [
                basis[2 * q].reshape(kinds * BLOCK, BLOCK),
                basis[2 * q + 1].reshape(kinds * BLOCK, BLOCK),
            ],
            axis=1,
        )
        product[q % 2] = jnp.dot(
            factors, placed[2 * q * BLOCK : 2 * (q + 1) * BLOCK, :], preferred_element_type=jnp.float32
        )
        for i in range(2):
            start = pl.multiple_of(scalars_ref[2 * q + i], BLOCK)
            for k in range(kinds):
                sums[pl.ds(start, BLOCK), k * BLOCK : (k + 1) * BLOCK] += product[
                    q % 2, k * BLOCK : (k + 1) * BLOCK, i * BLOCK : (i + 1) * BLOCK
                ]
    triplet[...] = sums[:edges, :].astype(jnp.bfloat16)

    live = scalars_ref[2 * pairs]
    out_copies = []
    for n in range(chunks):
        span = slice(n * CHUNK, (n + 1) * CHUNK)
        if n % 2 == 0:
            for copy in part_copies[n : n + 2] + message_copies[n : n + 2]:
                copy.wait()
        fresh[n % 2] = jnp.dot(triplet[...], up[:, span], preferred_element_type=jnp.float32)
        for b in range(edges // ROWS):
            rows = slice(b * ROWS, (b + 1) * ROWS)
            low = fresh[n % 2, rows, :] + part[rows, span]
            total = (messages[rows, span].astype(jnp.float32) + low) + low * jnp.tanh(low)
            alive = lax.broadcasted_iota(jnp.int32, (ROWS, CHUNK), 0) < live - b * ROWS
            result[rows, span] = jnp.where(alive, total, 0.0).astype(jnp.bfloat16)
        copy = pltpu.make_async_copy(
            result.at[:, spans[n]], out_hbm.at[:, spans[n]], out_sem.at[n]
        )
        copy.start()
        out_copies.append(copy)
    for copy in out_copies:
        copy.wait()


def finish(scalars, rows, part, messages, basis, up):
    edges, width = messages.shape
    pairs, kinds = basis.shape[:2]
    inner = kinds * BLOCK
    chunks = width // CHUNK
    hbm = pl.BlockSpec(memory_space=pltpu.HBM)
    vmem = pl.BlockSpec(memory_space=pltpu.VMEM)
    return pl.pallas_call(
        finish_kernel,
        out_shape=jax.ShapeDtypeStruct((edges, width), jnp.bfloat16),
        in_specs=[pl.BlockSpec(memory_space=pltpu.SMEM)] + [hbm] * 3 + [vmem] * 2,
        out_specs=hbm,
        scratch_shapes=[
            pltpu.VMEM((edges, width), jnp.float32),
            pltpu.VMEM((edges, width), jnp.bfloat16),
            pltpu.VMEM((pairs * BLOCK, 2 * BLOCK), jnp.bfloat16),
            pltpu.VMEM((edges + BLOCK, inner), jnp.float32),
            pltpu.VMEM((edges, inner), jnp.bfloat16),
            pltpu.VMEM((2, inner, 2 * BLOCK), jnp.float32),
            pltpu.VMEM((2, edges, CHUNK), jnp.float32),
            pltpu.VMEM((edges, width), jnp.bfloat16),
            pltpu.SemaphoreType.DMA((pairs,)),
            pltpu.SemaphoreType.DMA((chunks,)),
            pltpu.SemaphoreType.DMA((chunks,)),
            pltpu.SemaphoreType.DMA((chunks,)),
        ],
        compiler_params=pltpu.CompilerParams(vmem_limit_bytes=12 << 20),
        cost_estimate=pl.CostEstimate(
            flops=700_000_000, bytes_accessed=7_000_000, transcendentals=600_000
        ),
        name="finish",
    )(
        scalars,
        *placed_in(pltpu.HBM, rows, part, messages),
        *placed_in(pltpu.VMEM, basis, up),
    )


def on_device(
    messages,
    edge_count,
    reverse,
    target_atom,
    pair_target,
    pair_source,
    pair_count,
    basis_blocks,
    trip_weight,
    up_weight,
    atom_first,
    atom_second,
):
    edges = messages.shape[0]
    width = trip_weight.shape[1]
    live_rows = lax.broadcasted_iota(jnp.int32, (edges, 1), 0) < edge_count[0]
    masked = jnp.where(live_rows, messages, jnp.zeros((), jnp.bfloat16))
    projected = jnp.dot(masked, trip_weight, preferred_element_type=jnp.float32).astype(
        jnp.bfloat16
    )
    both = lax.all_gather(projected, "xh", axis=0, tiled=True)
    tile_rows = lax.all_gather(both, "z", axis=0, tiled=True)
    tile_blocks = tile_rows.reshape(-1, BLOCK, width)
    atom_ids = lax.broadcasted_iota(jnp.int32, (1, A_DST), 1)
    one_hot = (target_atom[:, None] == atom_ids).astype(jnp.bfloat16)
    local_sums = lax.dot_general(
        one_hot, masked, (((0,), (0,)), ((), ())), preferred_element_type=jnp.float32
    ).astype(jnp.bfloat16)
    columns = atom_first.shape[1]
    first, both, local_sums = lax.optimization_barrier((atom_first.T, both, local_sums))
    first = shift_along_z(first, FIRST)
    parts = exchange(local_sums, SRC)
    sums = jnp.sum(parts.reshape(N_SRC, A_DST // N_SRC, -1).astype(jnp.float32), axis=0)
    scale = lax.rsqrt(jnp.mean(sums * sums, axis=-1, keepdims=True) + eps)
    normed = silu(sums * scale).astype(jnp.bfloat16)
    second, normed = lax.optimization_barrier((atom_second.T, normed))
    normed = spread(normed).reshape(N_XH * A_DST, -1)
    second = shift_along_z(second, SECOND)
    hidden = lax.dot_general(
        first, normed, (((1,), (1,)), ((), ())), preferred_element_type=jnp.float32
    )
    hidden, second = lax.optimization_barrier((silu(hidden).astype(jnp.bfloat16), second))
    hidden = spread(hidden)
    atoms = exchange(second_layer(column_order(FIRST), hidden, second), SHARERS)
    mirrored = jnp.take(projected, reverse[0], axis=0)
    blocks = edges // BLOCK
    inner = up_weight.shape[0] - width
    part, basis_blocks = edge_part(
        column_order(SECOND),
        atoms,
        mirrored,
        target_atom.reshape(blocks, BLOCK),
        up_weight[inner:],
        basis_blocks,
    )
    half_up = up_weight[:inner] * jnp.asarray(0.5, jnp.bfloat16)
    pairs = pair_target.shape[1]
    live_pairs = jnp.arange(pairs, dtype=jnp.int32) < pair_count[0]
    starts = jnp.where(live_pairs, pair_target[0], blocks) * BLOCK
    holder, local = pair_source[0] // blocks, pair_source[0] % blocks
    sources = ((holder % N_Z) * N_XH + holder // N_Z) * blocks + local
    scalars = jnp.concatenate([starts, sources, edge_count])
    return finish(scalars, tile_blocks, part, messages, basis_blocks, half_up)


def solution(mesh):
    split = Mesh(mesh.devices.reshape([n for _, n in AXES]), ALL)
    return jax.shard_map(
        on_device,
        mesh=split,
        in_specs=(
            P(ALL, None),
            P(ALL),
            P(ALL, None),
            P(ALL),
            P(ALL, None),
            P(ALL, None),
            P(ALL),
            P(ALL, None, None, None),
            P(),
            P(),
            P(None, ("xh", "z")),
            P(None, ("xh", "z")),
        ),
        out_specs=P(ALL, None),
        check_vma=False,
    )
```

```python
import jax
import jax.numpy as jnp
from jax import lax
from jax.experimental import pallas as pl
from jax.experimental.pallas import tpu as pltpu
from jax.sharding import Mesh, PartitionSpec as P

A_DST = 128
BLOCK = 128
CHUNK = 256
ROWS = 64
AXES = (("y", 4), ("xl", 2), ("c", 2), ("xh", 2), ("z", 16))
ALL = tuple(name for name, _ in AXES)
SRC = ("y", "xl", "c")
N_SRC = 16
N_XH = 2
N_Z = 16
SHIFTS = (0, 8, 1, -7, -1, 7, 2, -6, -2, 6, 3, -5, -3, 5, 4, -4)
SHARERS = ("xh", *SRC)
eps = 1e-06


def silu(values):
    return values / (1.0 + jnp.exp(-values))


def shift_along_z(columns):
    pairs = [
        (r * N_Z + (z + SHIFTS[r]) % N_Z, r * N_Z + z) for r in range(N_SRC) for z in range(N_Z)
    ]
    return lax.ppermute(columns, (*SRC, "z"), pairs)


def column_order():
    away = jnp.mod(jnp.arange(N_Z, dtype=jnp.int32) - lax.axis_index("z"), N_Z)
    places = [s % N_Z for s in SHIFTS]
    holders = jnp.asarray([places.index(d) for d in range(N_Z)], jnp.int32)[away]
    return jnp.concatenate([holders + h * N_SRC for h in range(N_XH)])


def placed_in(space, *arrays):
    return [pltpu.with_memory_space_constraint(x, space) for x in arrays]


def exchange(blocks, axes):
    return lax.all_to_all(blocks, axes, split_axis=0, concat_axis=0, tiled=True)


def spread(block):
    return exchange(jnp.broadcast_to(block[None], (N_XH * N_SRC, *block.shape)), SHARERS)


def second_layer(order, hidden, weight):
    def kernel(order_ref, hidden_ref, weight_ref, out_ref, sorted_ref):
        width = hidden_ref.shape[1]
        for i in range(N_XH * N_Z):
            sorted_ref[i * width : (i + 1) * width, :] = hidden_ref[order_ref[i]]
        out = jnp.dot(weight_ref[...], sorted_ref[...], preferred_element_type=jnp.float32).astype(
            jnp.bfloat16
        )
        for h in range(N_XH):
            block = out[:, h * A_DST : (h + 1) * A_DST]
            for r in range(N_SRC):
                out_ref[h * N_SRC + r] = block

    columns, features = weight.shape
    vmem = pl.BlockSpec(memory_space=pltpu.VMEM)
    return pl.pallas_call(
        kernel,
        out_shape=jax.ShapeDtypeStruct((N_XH * N_SRC, columns, A_DST), jnp.bfloat16),
        in_specs=[pl.BlockSpec(memory_space=pltpu.SMEM), vmem, vmem],
        out_specs=vmem,
        scratch_shapes=[pltpu.VMEM((features, N_XH * A_DST), jnp.bfloat16)],
        cost_estimate=pl.CostEstimate(
            flops=2 * 32 * 256 * 1024, bytes_accessed=700_000, transcendentals=0
        ),
        compiler_params=pltpu.CompilerParams(vmem_limit_bytes=8 << 20),
        name="second_layer",
    )(order, *placed_in(pltpu.VMEM, hidden, weight))


def edge_part(order, atoms, mirrored, targets, up, basis):
    def kernel(
        order_ref,
        atoms_ref,
        mirrored_ref,
        targets_ref,
        up_ref,
        basis_hbm,
        out_hbm,
        basis_ref,
        sorted_ref,
        hot,
        part,
        basis_sem,
        sems,
    ):
        copies = [pltpu.make_async_copy(basis_hbm, basis_ref, basis_sem)]
        copies[0].start()
        half = atoms_ref.shape[1]
        edges, width = part.shape
        for i in range(N_XH * N_Z):
            sorted_ref[i * half : (i + 1) * half, :] = atoms_ref[order_ref[i]]
        atom_ids = lax.broadcasted_iota(jnp.int32, (A_DST, BLOCK), 0)
        for b in range(edges // BLOCK):
            flags = (atom_ids == targets_ref[b : b + 1, :]).astype(jnp.float32)
            hot[b * BLOCK : (b + 1) * BLOCK, :] = flags.T.astype(jnp.bfloat16)
        for n in range(width // CHUNK):
            span = slice(n * CHUNK, (n + 1) * CHUNK)
            both = jnp.dot(mirrored_ref[...], up_ref[:, span], preferred_element_type=jnp.float32)
            both += lax.dot_general(
                hot[...],
                sorted_ref[span, :],
                (((1,), (1,)), ((), ())),
                preferred_element_type=jnp.float32,
            )
            part[:, span] = 0.5 * both
            columns = pl.ds(n * CHUNK, CHUNK)
            copies.append(
                pltpu.make_async_copy(part.at[:, columns], out_hbm.at[:, columns], sems.at[n])
            )
            copies[-1].start()
        for copy in copies:
            copy.wait()

    edges, width = mirrored.shape[0], up.shape[1]
    vmem = pl.BlockSpec(memory_space=pltpu.VMEM)
    hbm = pl.BlockSpec(memory_space=pltpu.HBM)
    return pl.pallas_call(
        kernel,
        out_shape=(
            pltpu.HBM((edges, width), jnp.float32),
            pltpu.VMEM(basis.shape, basis.dtype),
        ),
        in_specs=[pl.BlockSpec(memory_space=pltpu.SMEM)] + [vmem] * 4 + [hbm],
        out_specs=(hbm, vmem),
        scratch_shapes=[
            pltpu.VMEM((width, A_DST), jnp.bfloat16),
            pltpu.VMEM((edges, A_DST), jnp.bfloat16),
            pltpu.VMEM((edges, width), jnp.float32),
            pltpu.SemaphoreType.DMA,
            pltpu.SemaphoreType.DMA((width // CHUNK,)),
        ],
        cost_estimate=pl.CostEstimate(
            flops=270_000_000, bytes_accessed=5_000_000, transcendentals=0
        ),
        compiler_params=pltpu.CompilerParams(vmem_limit_bytes=12 << 20),
        name="edge_part",
    )(
        order,
        *placed_in(pltpu.VMEM, atoms, mirrored),
        targets,
        up,
        *placed_in(pltpu.HBM, basis),
    )


def finish_kernel(
    scalars_ref,
    rows_hbm,
    part_hbm,
    messages_hbm,
    basis,
    up,
    out_hbm,
    part,
    messages,
    placed,
    sums,
    triplet,
    product,
    fresh,
    result,
    row_sem,
    part_sem,
    message_sem,
    out_sem,
):
    pairs, kinds = basis.shape[0], basis.shape[1]
    edges, width = messages.shape
    chunks = width // CHUNK

    row_copies = [
        pltpu.make_async_copy(
            rows_hbm.at[scalars_ref[pairs + p]],
            placed.at[pl.ds(p * BLOCK, BLOCK), pl.ds(p % 2 * BLOCK, BLOCK)],
            row_sem.at[p],
        )
        for p in range(pairs)
    ]
    spans = [pl.ds(n * CHUNK, CHUNK) for n in range(chunks)]
    part_copies = [
        pltpu.make_async_copy(part_hbm.at[:, s], part.at[:, s], part_sem.at[n])
        for n, s in enumerate(spans)
    ]
    message_copies = [
        pltpu.make_async_copy(messages_hbm.at[:, s], messages.at[:, s], message_sem.at[n])
        for n, s in enumerate(spans)
    ]
    for copy in row_copies:
        copy.start()
    for first, second in zip(part_copies, message_copies):
        first.start()
        second.start()
    for p in range(pairs):
        off = (1 - p % 2) * BLOCK
        placed[p * BLOCK : (p + 1) * BLOCK, off : off + BLOCK] = jnp.zeros(
            (BLOCK, BLOCK), jnp.bfloat16
        )
    sums[...] = jnp.zeros_like(sums)

    for copy in row_copies:
        copy.wait()
    for q in range(pairs // 2):
        factors = jnp.concatenate(
            [
                basis[2 * q].reshape(kinds * BLOCK, BLOCK),
                basis[2 * q + 1].reshape(kinds * BLOCK, BLOCK),
            ],
            axis=1,
        )
        product[q % 2] = jnp.dot(
            factors, placed[2 * q * BLOCK : 2 * (q + 1) * BLOCK, :], preferred_element_type=jnp.float32
        )
        for i in range(2):
            start = pl.multiple_of(scalars_ref[2 * q + i], BLOCK)
            for k in range(kinds):
                sums[pl.ds(start, BLOCK), k * BLOCK : (k + 1) * BLOCK] += product[
                    q % 2, k * BLOCK : (k + 1) * BLOCK, i * BLOCK : (i + 1) * BLOCK
                ]
    triplet[...] = sums[:edges, :].astype(jnp.bfloat16)

    live = scalars_ref[2 * pairs]
    out_copies = []
    for n in range(chunks):
        span = slice(n * CHUNK, (n + 1) * CHUNK)
        if n % 2 == 0:
            for copy in part_copies[n : n + 2] + message_copies[n : n + 2]:
                copy.wait()
        fresh[n % 2] = jnp.dot(triplet[...], up[:, span], preferred_element_type=jnp.float32)
        for b in range(edges // ROWS):
            rows = slice(b * ROWS, (b + 1) * ROWS)
            low = fresh[n % 2, rows, :] + part[rows, span]
            total = (messages[rows, span].astype(jnp.float32) + low) + low * jnp.tanh(low)
            alive = lax.broadcasted_iota(jnp.int32, (ROWS, CHUNK), 0) < live - b * ROWS
            result[rows, span] = jnp.where(alive, total, 0.0).astype(jnp.bfloat16)
        copy = pltpu.make_async_copy(
            result.at[:, spans[n]], out_hbm.at[:, spans[n]], out_sem.at[n]
        )
        copy.start()
        out_copies.append(copy)
    for copy in out_copies:
        copy.wait()


def finish(scalars, rows, part, messages, basis, up):
    edges, width = messages.shape
    pairs, kinds = basis.shape[:2]
    inner = kinds * BLOCK
    chunks = width // CHUNK
    hbm = pl.BlockSpec(memory_space=pltpu.HBM)
    vmem = pl.BlockSpec(memory_space=pltpu.VMEM)
    return pl.pallas_call(
        finish_kernel,
        out_shape=jax.ShapeDtypeStruct((edges, width), jnp.bfloat16),
        in_specs=[pl.BlockSpec(memory_space=pltpu.SMEM)] + [hbm] * 3 + [vmem] * 2,
        out_specs=hbm,
        scratch_shapes=[
            pltpu.VMEM((edges, width), jnp.float32),
            pltpu.VMEM((edges, width), jnp.bfloat16),
            pltpu.VMEM((pairs * BLOCK, 2 * BLOCK), jnp.bfloat16),
            pltpu.VMEM((edges + BLOCK, inner), jnp.float32),
            pltpu.VMEM((edges, inner), jnp.bfloat16),
            pltpu.VMEM((2, inner, 2 * BLOCK), jnp.float32),
            pltpu.VMEM((2, edges, CHUNK), jnp.float32),
            pltpu.VMEM((edges, width), jnp.bfloat16),
            pltpu.SemaphoreType.DMA((pairs,)),
            pltpu.SemaphoreType.DMA((chunks,)),
            pltpu.SemaphoreType.DMA((chunks,)),
            pltpu.SemaphoreType.DMA((chunks,)),
        ],
        compiler_params=pltpu.CompilerParams(vmem_limit_bytes=12 << 20),
        cost_estimate=pl.CostEstimate(
            flops=700_000_000, bytes_accessed=7_000_000, transcendentals=600_000
        ),
        name="finish",
    )(
        scalars,
        *placed_in(pltpu.HBM, rows, part, messages),
        *placed_in(pltpu.VMEM, basis, up),
    )


def on_device(
    messages,
    edge_count,
    reverse,
    target_atom,
    pair_target,
    pair_source,
    pair_count,
    basis_blocks,
    trip_weight,
    up_weight,
    atom_first,
    atom_second,
):
    edges = messages.shape[0]
    width = trip_weight.shape[1]
    live_rows = lax.broadcasted_iota(jnp.int32, (edges, 1), 0) < edge_count[0]
    masked = jnp.where(live_rows, messages, jnp.zeros((), jnp.bfloat16))
    projected = jnp.dot(masked, trip_weight, preferred_element_type=jnp.float32).astype(
        jnp.bfloat16
    )
    both = lax.all_gather(projected, "xh", axis=0, tiled=True)
    tile_rows = lax.all_gather(both, "z", axis=0, tiled=True)
    tile_blocks = tile_rows.reshape(-1, BLOCK, width)
    columns = atom_first.shape[1]
    mine = jnp.concatenate([atom_first.T, atom_second.T], axis=0)
    mine, both = lax.optimization_barrier((mine, both))
    weights = shift_along_z(mine)
    first, second = weights[:columns], weights[columns:]
    order = column_order()
    atom_ids = lax.broadcasted_iota(jnp.int32, (1, A_DST), 1)
    one_hot = (target_atom[:, None] == atom_ids).astype(jnp.bfloat16)
    local_sums = lax.dot_general(
        one_hot, masked, (((0,), (0,)), ((), ())), preferred_element_type=jnp.float32
    ).astype(jnp.bfloat16)
    parts = exchange(local_sums, SRC)
    sums = jnp.sum(parts.reshape(N_SRC, A_DST // N_SRC, -1).astype(jnp.float32), axis=0)
    scale = lax.rsqrt(jnp.mean(sums * sums, axis=-1, keepdims=True) + eps)
    normed = silu(sums * scale).astype(jnp.bfloat16)
    normed = spread(normed).reshape(N_XH * A_DST, -1)
    hidden = lax.dot_general(
        first, normed, (((1,), (1,)), ((), ())), preferred_element_type=jnp.float32
    )
    hidden = spread(silu(hidden).astype(jnp.bfloat16))
    atoms = exchange(second_layer(order, hidden, second), SHARERS)
    mirrored = jnp.take(projected, reverse[0], axis=0)
    blocks = edges // BLOCK
    inner = up_weight.shape[0] - width
    part, basis_blocks = edge_part(
        order,
        atoms,
        mirrored,
        target_atom.reshape(blocks, BLOCK),
        up_weight[inner:],
        basis_blocks,
    )
    half_up = up_weight[:inner] * jnp.asarray(0.5, jnp.bfloat16)
    pairs = pair_target.shape[1]
    live_pairs = jnp.arange(pairs, dtype=jnp.int32) < pair_count[0]
    starts = jnp.where(live_pairs, pair_target[0], blocks) * BLOCK
    holder, local = pair_source[0] // blocks, pair_source[0] % blocks
    sources = ((holder % N_Z) * N_XH + holder // N_Z) * blocks + local
    scalars = jnp.concatenate([starts, sources, edge_count])
    return finish(scalars, tile_blocks, part, messages, basis_blocks, half_up)


def solution(mesh):
    split = Mesh(mesh.devices.reshape([n for _, n in AXES]), ALL)
    return jax.shard_map(
        on_device,
        mesh=split,
        in_specs=(
            P(ALL, None),
            P(ALL),
            P(ALL, None),
            P(ALL),
            P(ALL, None),
            P(ALL, None),
            P(ALL),
            P(ALL, None, None, None),
            P(),
            P(),
            P(None, ("xh", "z")),
            P(None, ("xh", "z")),
        ),
        out_specs=P(ALL, None),
        check_vma=False,
    )
```

```python
import jax
import jax.numpy as jnp
from jax import lax
from jax.experimental import pallas as pl
from jax.experimental.pallas import tpu as pltpu
from jax.sharding import Mesh, PartitionSpec as P

A_DST = 128
BLOCK = 128
CHUNK = 256
ROWS = 64
AXES = (("y", 4), ("xl", 2), ("c", 2), ("xh", 2), ("z", 16))
ALL = tuple(name for name, _ in AXES)
SRC = ("y", "xl", "c")
N_SRC = 16
N_XH = 2
N_Z = 16
SHIFTS = (0, 8, 1, -7, -1, 7, 2, -6, -2, 6, 3, -5, -3, 5, 4, -4)
SHARERS = ("xh", *SRC)
eps = 1e-06


def silu(values):
    return values / (1.0 + jnp.exp(-values))


def shift_along_z(columns):
    pairs = [
        (r * N_Z + (z + SHIFTS[r]) % N_Z, r * N_Z + z) for r in range(N_SRC) for z in range(N_Z)
    ]
    return lax.ppermute(columns, (*SRC, "z"), pairs)


def column_order():
    away = jnp.mod(jnp.arange(N_Z, dtype=jnp.int32) - lax.axis_index("z"), N_Z)
    places = [s % N_Z for s in SHIFTS]
    holders = jnp.asarray([places.index(d) for d in range(N_Z)], jnp.int32)[away]
    return jnp.concatenate([holders + h * N_SRC for h in range(N_XH)])


def placed_in(space, *arrays):
    return [pltpu.with_memory_space_constraint(x, space) for x in arrays]


def exchange(blocks, axes):
    return lax.all_to_all(blocks, axes, split_axis=0, concat_axis=0, tiled=True)


def spread(block):
    return exchange(jnp.broadcast_to(block[None], (N_XH * N_SRC, *block.shape)), SHARERS)


def second_layer(order, hidden, weight):
    def kernel(order_ref, hidden_ref, weight_ref, out_ref, sorted_ref):
        width = hidden_ref.shape[1]
        for i in range(N_XH * N_Z):
            sorted_ref[i * width : (i + 1) * width, :] = hidden_ref[order_ref[i]]
        out = jnp.dot(weight_ref[...], sorted_ref[...], preferred_element_type=jnp.float32).astype(
            jnp.bfloat16
        )
        for h in range(N_XH):
            block = out[:, h * A_DST : (h + 1) * A_DST]
            for r in range(N_SRC):
                out_ref[h * N_SRC + r] = block

    columns, features = weight.shape
    vmem = pl.BlockSpec(memory_space=pltpu.VMEM)
    return pl.pallas_call(
        kernel,
        out_shape=jax.ShapeDtypeStruct((N_XH * N_SRC, columns, A_DST), jnp.bfloat16),
        in_specs=[pl.BlockSpec(memory_space=pltpu.SMEM), vmem, vmem],
        out_specs=vmem,
        scratch_shapes=[pltpu.VMEM((features, N_XH * A_DST), jnp.bfloat16)],
        cost_estimate=pl.CostEstimate(
            flops=2 * 32 * 256 * 1024, bytes_accessed=700_000, transcendentals=0
        ),
        compiler_params=pltpu.CompilerParams(vmem_limit_bytes=8 << 20),
        name="second_layer",
    )(order, *placed_in(pltpu.VMEM, hidden, weight))


def edge_part(order, atoms, mirrored, targets, up, basis):
    def kernel(
        order_ref,
        atoms_ref,
        mirrored_ref,
        targets_ref,
        up_ref,
        basis_hbm,
        out_hbm,
        basis_ref,
        sorted_ref,
        hot,
        part,
        basis_sem,
        sems,
    ):
        copies = [pltpu.make_async_copy(basis_hbm, basis_ref, basis_sem)]
        copies[0].start()
        half = atoms_ref.shape[1]
        edges, width = part.shape
        for i in range(N_XH * N_Z):
            sorted_ref[i * half : (i + 1) * half, :] = atoms_ref[order_ref[i]]
        atom_ids = lax.broadcasted_iota(jnp.int32, (A_DST, BLOCK), 0)
        for b in range(edges // BLOCK):
            flags = (atom_ids == targets_ref[b : b + 1, :]).astype(jnp.float32)
            hot[b * BLOCK : (b + 1) * BLOCK, :] = flags.T.astype(jnp.bfloat16)
        for n in range(width // CHUNK):
            span = slice(n * CHUNK, (n + 1) * CHUNK)
            both = jnp.dot(mirrored_ref[...], up_ref[:, span], preferred_element_type=jnp.float32)
            both += lax.dot_general(
                hot[...],
                sorted_ref[span, :],
                (((1,), (1,)), ((), ())),
                preferred_element_type=jnp.float32,
            )
            part[:, span] = 0.5 * both
            columns = pl.ds(n * CHUNK, CHUNK)
            copies.append(
                pltpu.make_async_copy(part.at[:, columns], out_hbm.at[:, columns], sems.at[n])
            )
            copies[-1].start()
        for copy in copies:
            copy.wait()

    edges, width = mirrored.shape[0], up.shape[1]
    vmem = pl.BlockSpec(memory_space=pltpu.VMEM)
    hbm = pl.BlockSpec(memory_space=pltpu.HBM)
    return pl.pallas_call(
        kernel,
        out_shape=(
            pltpu.HBM((edges, width), jnp.float32),
            pltpu.VMEM(basis.shape, basis.dtype),
        ),
        in_specs=[pl.BlockSpec(memory_space=pltpu.SMEM)] + [vmem] * 4 + [hbm],
        out_specs=(hbm, vmem),
        scratch_shapes=[
            pltpu.VMEM((width, A_DST), jnp.bfloat16),
            pltpu.VMEM((edges, A_DST), jnp.bfloat16),
            pltpu.VMEM((edges, width), jnp.float32),
            pltpu.SemaphoreType.DMA,
            pltpu.SemaphoreType.DMA((width // CHUNK,)),
        ],
        cost_estimate=pl.CostEstimate(
            flops=270_000_000, bytes_accessed=5_000_000, transcendentals=0
        ),
        compiler_params=pltpu.CompilerParams(vmem_limit_bytes=12 << 20),
        name="edge_part",
    )(
        order,
        *placed_in(pltpu.VMEM, atoms, mirrored),
        targets,
        up,
        *placed_in(pltpu.HBM, basis),
    )


def finish_kernel(
    scalars_ref,
    rows_hbm,
    part_hbm,
    messages_hbm,
    basis,
    up,
    out_hbm,
    part,
    messages,
    placed,
    sums,
    triplet,
    fresh,
    result,
    row_sem,
    part_sem,
    message_sem,
    out_sem,
):
    pairs, kinds = basis.shape[0], basis.shape[1]
    edges, width = messages.shape
    chunks = width // CHUNK

    row_copies = [
        pltpu.make_async_copy(
            rows_hbm.at[scalars_ref[pairs + p]],
            placed.at[pl.ds(p * BLOCK, BLOCK), pl.ds(p % 2 * BLOCK, BLOCK)],
            row_sem.at[p],
        )
        for p in range(pairs)
    ]
    spans = [pl.ds(n * CHUNK, CHUNK) for n in range(chunks)]
    part_copies = [
        pltpu.make_async_copy(part_hbm.at[:, s], part.at[:, s], part_sem.at[n])
        for n, s in enumerate(spans)
    ]
    message_copies = [
        pltpu.make_async_copy(messages_hbm.at[:, s], messages.at[:, s], message_sem.at[n])
        for n, s in enumerate(spans)
    ]
    for copy in row_copies:
        copy.start()
    for first, second in zip(part_copies, message_copies):
        first.start()
        second.start()
    for p in range(pairs):
        off = (1 - p % 2) * BLOCK
        placed[p * BLOCK : (p + 1) * BLOCK, off : off + BLOCK] = jnp.zeros(
            (BLOCK, BLOCK), jnp.bfloat16
        )
    sums[...] = jnp.zeros_like(sums)

    for copy in row_copies:
        copy.wait()
    for q in range(pairs // 2):
        block = placed[2 * q * BLOCK : 2 * (q + 1) * BLOCK, :]
        starts = [pl.multiple_of(scalars_ref[2 * q + i], BLOCK) for i in range(2)]
        for k in range(kinds):
            product = jnp.dot(
                jnp.concatenate([basis[2 * q, k], basis[2 * q + 1, k]], axis=1),
                block,
                preferred_element_type=jnp.float32,
            )
            for i in range(2):
                sums[pl.ds(starts[i], BLOCK), k * BLOCK : (k + 1) * BLOCK] += product[
                    :, i * BLOCK : (i + 1) * BLOCK
                ]
    triplet[...] = sums[:edges, :].astype(jnp.bfloat16)

    live = scalars_ref[2 * pairs]
    out_copies = []
    for n in range(chunks):
        span = slice(n * CHUNK, (n + 1) * CHUNK)
        if n % 2 == 0:
            for copy in part_copies[n : n + 2] + message_copies[n : n + 2]:
                copy.wait()
        fresh[n % 2] = jnp.dot(triplet[...], up[:, span], preferred_element_type=jnp.float32)
        for b in range(edges // ROWS):
            rows = slice(b * ROWS, (b + 1) * ROWS)
            low = fresh[n % 2, rows, :] + part[rows, span]
            total = messages[rows, span].astype(jnp.float32) + (low + low * jnp.tanh(low))
            alive = lax.broadcasted_iota(jnp.int32, (ROWS, CHUNK), 0) < live - b * ROWS
            result[rows, span] = jnp.where(
                alive, total.astype(jnp.bfloat16), jnp.zeros((), jnp.bfloat16)
            )
        copy = pltpu.make_async_copy(
            result.at[:, spans[n]], out_hbm.at[:, spans[n]], out_sem.at[n]
        )
        copy.start()
        out_copies.append(copy)
    for copy in out_copies:
        copy.wait()


def finish(scalars, rows, part, messages, basis, up):
    edges, width = messages.shape
    pairs, kinds = basis.shape[:2]
    inner = kinds * BLOCK
    chunks = width // CHUNK
    hbm = pl.BlockSpec(memory_space=pltpu.HBM)
    vmem = pl.BlockSpec(memory_space=pltpu.VMEM)
    return pl.pallas_call(
        finish_kernel,
        out_shape=jax.ShapeDtypeStruct((edges, width), jnp.bfloat16),
        in_specs=[pl.BlockSpec(memory_space=pltpu.SMEM)] + [hbm] * 3 + [vmem] * 2,
        out_specs=hbm,
        scratch_shapes=[
            pltpu.VMEM((edges, width), jnp.float32),
            pltpu.VMEM((edges, width), jnp.bfloat16),
            pltpu.VMEM((pairs * BLOCK, 2 * BLOCK), jnp.bfloat16),
            pltpu.VMEM((edges + BLOCK, inner), jnp.float32),
            pltpu.VMEM((edges, inner), jnp.bfloat16),
            pltpu.VMEM((2, edges, CHUNK), jnp.float32),
            pltpu.VMEM((edges, width), jnp.bfloat16),
            pltpu.SemaphoreType.DMA((pairs,)),
            pltpu.SemaphoreType.DMA((chunks,)),
            pltpu.SemaphoreType.DMA((chunks,)),
            pltpu.SemaphoreType.DMA((chunks,)),
        ],
        compiler_params=pltpu.CompilerParams(vmem_limit_bytes=12 << 20),
        cost_estimate=pl.CostEstimate(
            flops=700_000_000, bytes_accessed=7_000_000, transcendentals=600_000
        ),
        name="finish",
    )(
        scalars,
        *placed_in(pltpu.HBM, rows, part, messages),
        *placed_in(pltpu.VMEM, basis, up),
    )


def on_device(
    messages,
    edge_count,
    reverse,
    target_atom,
    pair_target,
    pair_source,
    pair_count,
    basis_blocks,
    trip_weight,
    up_weight,
    atom_first,
    atom_second,
):
    edges = messages.shape[0]
    width = trip_weight.shape[1]
    live_rows = lax.broadcasted_iota(jnp.int32, (edges, 1), 0) < edge_count[0]
    masked = jnp.where(live_rows, messages, jnp.zeros((), jnp.bfloat16))
    projected = jnp.dot(masked, trip_weight, preferred_element_type=jnp.float32).astype(
        jnp.bfloat16
    )
    both = lax.all_gather(projected, "xh", axis=0, tiled=True)
    tile_rows = lax.all_gather(both, "z", axis=0, tiled=True)
    tile_blocks = tile_rows.reshape(-1, BLOCK, width)
    columns = atom_first.shape[1]
    mine = jnp.concatenate([atom_first.T, atom_second.T], axis=0)
    mine, both = lax.optimization_barrier((mine, both))
    weights = shift_along_z(mine)
    first, second = weights[:columns], weights[columns:]
    order = column_order()
    atom_ids = lax.broadcasted_iota(jnp.int32, (1, A_DST), 1)
    one_hot = (target_atom[:, None] == atom_ids).astype(jnp.bfloat16)
    local_sums = lax.dot_general(
        one_hot, masked, (((0,), (0,)), ((), ())), preferred_element_type=jnp.float32
    ).astype(jnp.bfloat16)
    parts = exchange(local_sums, SRC)
    sums = jnp.sum(parts.reshape(N_SRC, A_DST // N_SRC, -1).astype(jnp.float32), axis=0)
    scale = lax.rsqrt(jnp.mean(sums * sums, axis=-1, keepdims=True) + eps)
    normed = silu(sums * scale).astype(jnp.bfloat16)
    normed = spread(normed).reshape(N_XH * A_DST, -1)
    hidden = lax.dot_general(
        first, normed, (((1,), (1,)), ((), ())), preferred_element_type=jnp.float32
    )
    hidden = spread(silu(hidden).astype(jnp.bfloat16))
    atoms = exchange(second_layer(order, hidden, second), SHARERS)
    mirrored = jnp.take(projected, reverse[0], axis=0)
    blocks = edges // BLOCK
    inner = up_weight.shape[0] - width
    part, basis_blocks = edge_part(
        order,
        atoms,
        mirrored,
        target_atom.reshape(blocks, BLOCK),
        up_weight[inner:],
        basis_blocks,
    )
    half_up = up_weight[:inner] * jnp.asarray(0.5, jnp.bfloat16)
    pairs = pair_target.shape[1]
    live_pairs = jnp.arange(pairs, dtype=jnp.int32) < pair_count[0]
    starts = jnp.where(live_pairs, pair_target[0], blocks) * BLOCK
    holder, local = pair_source[0] // blocks, pair_source[0] % blocks
    sources = ((holder % N_Z) * N_XH + holder // N_Z) * blocks + local
    scalars = jnp.concatenate([starts, sources, edge_count])
    return finish(scalars, tile_blocks, part, messages, basis_blocks, half_up)


def solution(mesh):
    split = Mesh(mesh.devices.reshape([n for _, n in AXES]), ALL)
    return jax.shard_map(
        on_device,
        mesh=split,
        in_specs=(
            P(ALL, None),
            P(ALL),
            P(ALL, None),
            P(ALL),
            P(ALL, None),
            P(ALL, None),
            P(ALL),
            P(ALL, None, None, None),
            P(),
            P(),
            P(None, ("xh", "z")),
            P(None, ("xh", "z")),
        ),
        out_specs=P(ALL, None),
        check_vma=False,
    )
```

```python
import jax
import jax.numpy as jnp
from jax import lax
from jax.experimental import pallas as pl
from jax.experimental.pallas import tpu as pltpu
from jax.sharding import Mesh, PartitionSpec as P

A_DST = 128
BLOCK = 128
CHUNK = 256
ROWS = 64
AXES = (("y", 4), ("xl", 2), ("c", 2), ("xh", 2), ("z", 16))
ALL = tuple(name for name, _ in AXES)
SRC = ("y", "xl", "c")
N_SRC = 16
N_XH = 2
N_Z = 16
SHIFTS = (0, 8, 1, -7, -1, 7, 2, -6, -2, 6, 3, -5, -3, 5, 4, -4)
SHARERS = ("xh", *SRC)
eps = 1e-06


def silu(values):
    return values / (1.0 + jnp.exp(-values))


def shift_along_z(columns):
    pairs = [
        (r * N_Z + (z + SHIFTS[r]) % N_Z, r * N_Z + z) for r in range(N_SRC) for z in range(N_Z)
    ]
    return lax.ppermute(columns, (*SRC, "z"), pairs)


def column_order():
    away = jnp.mod(jnp.arange(N_Z, dtype=jnp.int32) - lax.axis_index("z"), N_Z)
    places = [s % N_Z for s in SHIFTS]
    holders = jnp.asarray([places.index(d) for d in range(N_Z)], jnp.int32)[away]
    return jnp.concatenate([holders + h * N_SRC for h in range(N_XH)])


def placed_in(space, *arrays):
    return [pltpu.with_memory_space_constraint(x, space) for x in arrays]


def exchange(blocks, axes):
    return lax.all_to_all(blocks, axes, split_axis=0, concat_axis=0, tiled=True)


def spread(block):
    return exchange(jnp.broadcast_to(block[None], (N_XH * N_SRC, *block.shape)), SHARERS)


def second_layer(order, hidden, weight):
    def kernel(order_ref, hidden_ref, weight_ref, out_ref, sorted_ref):
        width = hidden_ref.shape[1]
        for i in range(N_XH * N_Z):
            sorted_ref[i * width : (i + 1) * width, :] = hidden_ref[order_ref[i]]
        out = jnp.dot(weight_ref[...], sorted_ref[...], preferred_element_type=jnp.float32).astype(
            jnp.bfloat16
        )
        for h in range(N_XH):
            block = out[:, h * A_DST : (h + 1) * A_DST]
            for r in range(N_SRC):
                out_ref[h * N_SRC + r] = block

    columns, features = weight.shape
    vmem = pl.BlockSpec(memory_space=pltpu.VMEM)
    return pl.pallas_call(
        kernel,
        out_shape=jax.ShapeDtypeStruct((N_XH * N_SRC, columns, A_DST), jnp.bfloat16),
        in_specs=[pl.BlockSpec(memory_space=pltpu.SMEM), vmem, vmem],
        out_specs=vmem,
        scratch_shapes=[pltpu.VMEM((features, N_XH * A_DST), jnp.bfloat16)],
        cost_estimate=pl.CostEstimate(
            flops=2 * 32 * 256 * 1024, bytes_accessed=700_000, transcendentals=0
        ),
        compiler_params=pltpu.CompilerParams(vmem_limit_bytes=8 << 20),
        name="second_layer",
    )(order, *placed_in(pltpu.VMEM, hidden, weight))


def edge_part(order, atoms, mirrored, targets, up, basis):
    def kernel(
        order_ref,
        atoms_ref,
        mirrored_ref,
        targets_ref,
        up_ref,
        basis_hbm,
        out_hbm,
        basis_ref,
        sorted_ref,
        hot,
        part,
        basis_sem,
        sems,
    ):
        copies = [pltpu.make_async_copy(basis_hbm, basis_ref, basis_sem)]
        copies[0].start()
        half = atoms_ref.shape[1]
        edges, width = part.shape
        for i in range(N_XH * N_Z):
            sorted_ref[i * half : (i + 1) * half, :] = atoms_ref[order_ref[i]]
        atom_ids = lax.broadcasted_iota(jnp.int32, (A_DST, BLOCK), 0)
        for b in range(edges // BLOCK):
            flags = (atom_ids == targets_ref[b : b + 1, :]).astype(jnp.float32)
            hot[b * BLOCK : (b + 1) * BLOCK, :] = flags.T.astype(jnp.bfloat16)
        for n in range(width // CHUNK):
            span = slice(n * CHUNK, (n + 1) * CHUNK)
            both = jnp.dot(mirrored_ref[...], up_ref[:, span], preferred_element_type=jnp.float32)
            both += lax.dot_general(
                hot[...],
                sorted_ref[span, :],
                (((1,), (1,)), ((), ())),
                preferred_element_type=jnp.float32,
            )
            part[:, span] = 0.5 * both
            columns = pl.ds(n * CHUNK, CHUNK)
            copies.append(
                pltpu.make_async_copy(part.at[:, columns], out_hbm.at[:, columns], sems.at[n])
            )
            copies[-1].start()
        for copy in copies:
            copy.wait()

    edges, width = mirrored.shape[0], up.shape[1]
    vmem = pl.BlockSpec(memory_space=pltpu.VMEM)
    hbm = pl.BlockSpec(memory_space=pltpu.HBM)
    return pl.pallas_call(
        kernel,
        out_shape=(
            pltpu.HBM((edges, width), jnp.float32),
            pltpu.VMEM(basis.shape, basis.dtype),
        ),
        in_specs=[pl.BlockSpec(memory_space=pltpu.SMEM)] + [vmem] * 4 + [hbm],
        out_specs=(hbm, vmem),
        scratch_shapes=[
            pltpu.VMEM((width, A_DST), jnp.bfloat16),
            pltpu.VMEM((edges, A_DST), jnp.bfloat16),
            pltpu.VMEM((edges, width), jnp.float32),
            pltpu.SemaphoreType.DMA,
            pltpu.SemaphoreType.DMA((width // CHUNK,)),
        ],
        cost_estimate=pl.CostEstimate(
            flops=270_000_000, bytes_accessed=5_000_000, transcendentals=0
        ),
        compiler_params=pltpu.CompilerParams(vmem_limit_bytes=12 << 20),
        name="edge_part",
    )(
        order,
        *placed_in(pltpu.VMEM, atoms, mirrored),
        targets,
        up,
        *placed_in(pltpu.HBM, basis),
    )


def finish_kernel(
    scalars_ref,
    rows_hbm,
    part_hbm,
    messages_hbm,
    basis,
    up,
    out_hbm,
    part,
    messages,
    placed,
    sums,
    triplet,
    fresh,
    result,
    row_sem,
    part_sem,
    message_sem,
    out_sem,
):
    pairs, kinds = basis.shape[0], basis.shape[1]
    edges, width = messages.shape
    chunks = width // CHUNK

    row_copies = [
        pltpu.make_async_copy(
            rows_hbm.at[scalars_ref[pairs + p]],
            placed.at[pl.ds(p * BLOCK, BLOCK), pl.ds(p % 2 * BLOCK, BLOCK)],
            row_sem.at[p],
        )
        for p in range(pairs)
    ]
    spans = [pl.ds(n * CHUNK, CHUNK) for n in range(chunks)]
    part_copies = [
        pltpu.make_async_copy(part_hbm.at[:, s], part.at[:, s], part_sem.at[n])
        for n, s in enumerate(spans)
    ]
    message_copies = [
        pltpu.make_async_copy(messages_hbm.at[:, s], messages.at[:, s], message_sem.at[n])
        for n, s in enumerate(spans)
    ]
    for copy in row_copies:
        copy.start()
    for first, second in zip(part_copies, message_copies):
        first.start()
        second.start()
    for p in range(pairs):
        off = (1 - p % 2) * BLOCK
        placed[p * BLOCK : (p + 1) * BLOCK, off : off + BLOCK] = jnp.zeros(
            (BLOCK, BLOCK), jnp.bfloat16
        )
    sums[...] = jnp.zeros_like(sums)

    for copy in row_copies:
        copy.wait()
    for q in range(pairs // 2):
        block = placed[2 * q * BLOCK : 2 * (q + 1) * BLOCK, :]
        starts = [pl.multiple_of(scalars_ref[2 * q + i], BLOCK) for i in range(2)]
        for k in range(kinds):
            product = jnp.dot(
                jnp.concatenate([basis[2 * q, k], basis[2 * q + 1, k]], axis=1),
                block,
                preferred_element_type=jnp.float32,
            )
            for i in range(2):
                sums[pl.ds(starts[i], BLOCK), k * BLOCK : (k + 1) * BLOCK] += product[
                    :, i * BLOCK : (i + 1) * BLOCK
                ]
    triplet[...] = sums[:edges, :].astype(jnp.bfloat16)

    for copy in part_copies + message_copies:
        copy.wait()
    live = scalars_ref[2 * pairs]
    out_copies = []
    for n in range(chunks):
        span = slice(n * CHUNK, (n + 1) * CHUNK)
        fresh[n % 2] = jnp.dot(triplet[...], up[:, span], preferred_element_type=jnp.float32)
        for b in range(edges // ROWS):
            rows = slice(b * ROWS, (b + 1) * ROWS)
            low = fresh[n % 2, rows, :] + part[rows, span]
            total = messages[rows, span].astype(jnp.float32) + (low + low * jnp.tanh(low))
            alive = lax.broadcasted_iota(jnp.int32, (ROWS, CHUNK), 0) < live - b * ROWS
            result[rows, span] = jnp.where(
                alive, total.astype(jnp.bfloat16), jnp.zeros((), jnp.bfloat16)
            )
        copy = pltpu.make_async_copy(
            result.at[:, spans[n]], out_hbm.at[:, spans[n]], out_sem.at[n]
        )
        copy.start()
        out_copies.append(copy)
    for copy in out_copies:
        copy.wait()


def finish(scalars, rows, part, messages, basis, up):
    edges, width = messages.shape
    pairs, kinds = basis.shape[:2]
    inner = kinds * BLOCK
    chunks = width // CHUNK
    hbm = pl.BlockSpec(memory_space=pltpu.HBM)
    vmem = pl.BlockSpec(memory_space=pltpu.VMEM)
    return pl.pallas_call(
        finish_kernel,
        out_shape=jax.ShapeDtypeStruct((edges, width), jnp.bfloat16),
        in_specs=[pl.BlockSpec(memory_space=pltpu.SMEM)] + [hbm] * 3 + [vmem] * 2,
        out_specs=hbm,
        scratch_shapes=[
            pltpu.VMEM((edges, width), jnp.float32),
            pltpu.VMEM((edges, width), jnp.bfloat16),
            pltpu.VMEM((pairs * BLOCK, 2 * BLOCK), jnp.bfloat16),
            pltpu.VMEM((edges + BLOCK, inner), jnp.float32),
            pltpu.VMEM((edges, inner), jnp.bfloat16),
            pltpu.VMEM((2, edges, CHUNK), jnp.float32),
            pltpu.VMEM((edges, width), jnp.bfloat16),
            pltpu.SemaphoreType.DMA((pairs,)),
            pltpu.SemaphoreType.DMA((chunks,)),
            pltpu.SemaphoreType.DMA((chunks,)),
            pltpu.SemaphoreType.DMA((chunks,)),
        ],
        compiler_params=pltpu.CompilerParams(vmem_limit_bytes=12 << 20),
        cost_estimate=pl.CostEstimate(
            flops=700_000_000, bytes_accessed=7_000_000, transcendentals=600_000
        ),
        name="finish",
    )(
        scalars,
        *placed_in(pltpu.HBM, rows, part, messages),
        *placed_in(pltpu.VMEM, basis, up),
    )


def on_device(
    messages,
    edge_count,
    reverse,
    target_atom,
    pair_target,
    pair_source,
    pair_count,
    basis_blocks,
    trip_weight,
    up_weight,
    atom_first,
    atom_second,
):
    edges = messages.shape[0]
    width = trip_weight.shape[1]
    live_rows = lax.broadcasted_iota(jnp.int32, (edges, 1), 0) < edge_count[0]
    masked = jnp.where(live_rows, messages, jnp.zeros((), jnp.bfloat16))
    projected = jnp.dot(masked, trip_weight, preferred_element_type=jnp.float32).astype(
        jnp.bfloat16
    )
    both = lax.all_gather(projected, "xh", axis=0, tiled=True)
    tile_rows = lax.all_gather(both, "z", axis=0, tiled=True)
    tile_blocks = tile_rows.reshape(-1, BLOCK, width)
    columns = atom_first.shape[1]
    mine = jnp.concatenate([atom_first.T, atom_second.T], axis=0)
    mine, both = lax.optimization_barrier((mine, both))
    weights = shift_along_z(mine)
    first, second = weights[:columns], weights[columns:]
    order = column_order()
    atom_ids = lax.broadcasted_iota(jnp.int32, (1, A_DST), 1)
    one_hot = (target_atom[:, None] == atom_ids).astype(jnp.bfloat16)
    local_sums = lax.dot_general(
        one_hot, masked, (((0,), (0,)), ((), ())), preferred_element_type=jnp.float32
    ).astype(jnp.bfloat16)
    parts = exchange(local_sums, SRC)
    sums = jnp.sum(parts.reshape(N_SRC, A_DST // N_SRC, -1).astype(jnp.float32), axis=0)
    scale = lax.rsqrt(jnp.mean(sums * sums, axis=-1, keepdims=True) + eps)
    normed = silu(sums * scale).astype(jnp.bfloat16)
    normed = spread(normed).reshape(N_XH * A_DST, -1)
    hidden = lax.dot_general(
        first, normed, (((1,), (1,)), ((), ())), preferred_element_type=jnp.float32
    )
    hidden = spread(silu(hidden).astype(jnp.bfloat16))
    atoms = exchange(second_layer(order, hidden, second), SHARERS)
    mirrored = jnp.take(projected, reverse[0], axis=0)
    blocks = edges // BLOCK
    inner = up_weight.shape[0] - width
    part, basis_blocks = edge_part(
        order,
        atoms,
        mirrored,
        target_atom.reshape(blocks, BLOCK),
        up_weight[inner:],
        basis_blocks,
    )
    half_up = up_weight[:inner] * jnp.asarray(0.5, jnp.bfloat16)
    pairs = pair_target.shape[1]
    live_pairs = jnp.arange(pairs, dtype=jnp.int32) < pair_count[0]
    starts = jnp.where(live_pairs, pair_target[0], blocks) * BLOCK
    holder, local = pair_source[0] // blocks, pair_source[0] % blocks
    sources = ((holder % N_Z) * N_XH + holder // N_Z) * blocks + local
    scalars = jnp.concatenate([starts, sources, edge_count])
    return finish(scalars, tile_blocks, part, messages, basis_blocks, half_up)


def solution(mesh):
    split = Mesh(mesh.devices.reshape([n for _, n in AXES]), ALL)
    return jax.shard_map(
        on_device,
        mesh=split,
        in_specs=(
            P(ALL, None),
            P(ALL),
            P(ALL, None),
            P(ALL),
            P(ALL, None),
            P(ALL, None),
            P(ALL),
            P(ALL, None, None, None),
            P(),
            P(),
            P(None, ("xh", "z")),
            P(None, ("xh", "z")),
        ),
        out_specs=P(ALL, None),
        check_vma=False,
    )
```
